32 devices in a mesh: outer: 4 (over y, x), inner: 8 (over z, core).
Axes of the slice: x: 2, y: 2, z: 4, core: 2. Of those that a mesh axis runs over, the one named last changes fastest.
Arguments:
- query_rows: bfloat16 [6144, 384], P(('outer', 'inner')), may hold values from -6 to 6
- key_rows: bfloat16 [6144, 384], P(('outer', 'inner')), may hold values from -6 to 6
- value_rows: bfloat16 [6144, 384], P(('outer', 'inner')), may hold values from -6 to 6
- out_grad: bfloat16 [6144, 384], P(('outer', 'inner')), may hold values from -6 to 6
Outputs:
- attended: bfloat16 [6144, 384], P(('outer', 'inner'))
- d_query: bfloat16 [6144, 384], P(('outer', 'inner'))
- d_key: bfloat16 [6144, 384], P(('outer', 'inner'))
- d_value: bfloat16 [6144, 384], P(('outer', 'inner'))
The draws below stay inside these ranges and needn't reach their ends.
All inputs are finite; a program needn't handle non-finite values.
Results may differ from the reference program's by a relative error of at most 0.012.
The reference program's roundings to bfloat16 on the way count: a program that leaves them out, or rounds other values in their place, can miss the bound.
Values may be sent and summed in bfloat16 or wider, within the bound.
No kernel may reach another device: no remote copies, remote signals or barrier semaphores. Data moves between devices by JAX's collectives and lax.ppermute only.
A program may use at most 64 MiB of HBM per device.

```python
import jax
import jax.numpy as jnp
import numpy as np
from jax import lax

HEADS = 6
HEAD_DIM = 64
TOKENS = 6144
SEG_A = 1536
SEG_B = 3072


def draw_query_rows(key, part):
    values = jnp.clip(1.5 * jax.random.normal(jax.random.fold_in(key, 1), (TOKENS, HEADS, HEAD_DIM), jnp.float32), -6.0, 6.0)
    return values.reshape(TOKENS, HEADS * HEAD_DIM).astype(jnp.bfloat16)


def draw_key_rows(key, part):
    values = jnp.clip(1.5 * jax.random.normal(jax.random.fold_in(key, 2), (TOKENS, HEADS, HEAD_DIM), jnp.float32), -6.0, 6.0)
    return values.reshape(TOKENS, HEADS * HEAD_DIM).astype(jnp.bfloat16)


def level_of(stream_key, shape, cuts, low, high):
    gain, own = 1.0, jax.random.fold_in(stream_key, 6)
    for axis_at, shards_of in cuts:
        steps = jnp.exp(jax.random.uniform(jax.random.fold_in(own, axis_at), (shards_of,), jnp.float32, low / len(cuts), high / len(cuts)))
        gain = gain * jnp.repeat(steps, shape[axis_at] // shards_of).reshape([-1 if axis == axis_at else 1 for axis in range(len(shape))])
    return gain


def noise(rng, shape, deviation, most, shards=(), held_as=jnp.bfloat16):
    values = deviation * jax.random.normal(rng, shape, jnp.float32)
    if shards:
        values = values * level_of(rng, shape, shards, -0.22, 0.18)
    return jnp.clip(values, -most, most).astype(held_as)


def setup_inputs(seed: int = 0) -> dict:
    arg_keys = jax.random.split(jax.random.key(seed), 5)
    return {
        "query_rows": draw_query_rows(jax.random.fold_in(arg_keys[4], 71), 0),
        "key_rows": draw_key_rows(jax.random.fold_in(arg_keys[4], 71), 0),
        "value_rows": noise(arg_keys[2], (TOKENS, HEADS * HEAD_DIM), 1.0, 6.0, ((0, 32),)),
        "out_grad": noise(arg_keys[3], (TOKENS, HEADS * HEAD_DIM), 1.0, 6.0, ((0, 32),)),
    }


def pick_rows(source, stride, offsets):
    head_count = source.shape[1]
    shaped = source.reshape((source.shape[0] // stride, stride) + source.shape[1:])
    return shaped[:, offsets, np.arange(head_count)]

def spread_rows(chosen, stride, offsets):
    head_count = chosen.shape[1]
    selector = (np.arange(stride)[:, None] == offsets[None, :]).reshape((1, stride, head_count) + (1,) * (chosen.ndim - 2))
    widened = jnp.where(selector, chosen[:, None], jnp.zeros((), chosen.dtype))
    return widened.reshape((chosen.shape[0] * stride,) + chosen.shape[1:])

def head_forward(query_head, key_head, value_head, scaling):
    scores = jnp.dot(query_head, key_head.T, preferred_element_type=jnp.float32) * scaling
    highest = lax.optimization_barrier(jnp.max(scores, axis=1))
    levels = highest + jnp.log(lax.optimization_barrier(jnp.sum(jnp.exp(scores - highest[:, None]), axis=1)))
    weights_low = jnp.exp(scores - levels[:, None]).astype(jnp.bfloat16)
    return (levels, jnp.dot(weights_low, value_head, preferred_element_type=jnp.float32))

def head_query_grad(query_head, key_head, value_head, grad_head, corr_head, level_head, scaling):
    scores = jnp.dot(query_head, key_head.T, preferred_element_type=jnp.float32) * scaling
    redone = jnp.exp(scores - level_head[:, None])
    dprob = jnp.dot(grad_head, value_head.T, preferred_element_type=jnp.float32)
    dscore = (redone * (dprob - corr_head[:, None])).astype(jnp.bfloat16)
    return (jnp.dot(dscore, key_head, preferred_element_type=jnp.float32) * scaling,)

def head_key_grad(key_head, value_head, query_head, grad_head, corr_head, level_head, scaling):
    scores = jnp.dot(key_head, query_head.T, preferred_element_type=jnp.float32) * scaling
    redone = jnp.exp(scores - level_head[None, :])
    value_grad = jnp.dot(redone.astype(jnp.bfloat16), grad_head, preferred_element_type=jnp.float32)
    dprob = jnp.dot(value_head, grad_head.T, preferred_element_type=jnp.float32)
    dscore = (redone * (dprob - corr_head[None, :])).astype(jnp.bfloat16)
    return (jnp.dot(dscore, query_head, preferred_element_type=jnp.float32) * scaling, value_grad)

def over_heads(kernel, arrays):

    def one_head(head_index):
        return kernel(*[lax.dynamic_index_in_dim(member, head_index, 1, keepdims=False) for member in arrays])
    results = lax.map(one_head, jnp.arange(arrays[0].shape[1], dtype=jnp.int32))
    return tuple((jnp.moveaxis(member, 0, 1) for member in results))

def attend(queries, keys_in, values_in, scaling):

    def kernel(query_head, key_head, value_head):
        return head_forward(query_head, key_head, value_head, scaling)
    return over_heads(kernel, (queries, keys_in, values_in))

def query_grads(queries, keys_in, values_in, grads_in, corrs_in, levels_in, scaling):

    def kernel(query_head, key_head, value_head, grad_head, corr_head, level_head):
        return head_query_grad(query_head, key_head, value_head, grad_head, corr_head, level_head, scaling)
    return over_heads(kernel, (queries, keys_in, values_in, grads_in, corrs_in, levels_in))[0]

def key_grads(keys_in, values_in, queries, grads_in, corrs_in, levels_in, scaling):

    def kernel(key_head, value_head, query_head, grad_head, corr_head, level_head):
        return head_key_grad(key_head, value_head, query_head, grad_head, corr_head, level_head, scaling)
    return over_heads(kernel, (keys_in, values_in, queries, grads_in, corrs_in, levels_in))

def combine(levels, branch_outs, masks):
    base = levels[0]
    highest = base
    for branch_level, member_mask in zip(levels[1:], masks[1:]):
        highest = jnp.maximum(highest, jnp.where(member_mask, branch_level, base))
    totals = jnp.zeros_like(base)
    for branch_level, member_mask in zip(levels, masks):
        totals = totals + jnp.where(member_mask, jnp.exp(branch_level - highest), 0.0)
    overall = highest + jnp.log(totals)
    weights = [jnp.where(member_mask, jnp.exp(branch_level - overall), 0.0) for branch_level, member_mask in zip(levels, masks)]
    combined = jnp.zeros_like(branch_outs[0])
    for weight, branch_out in zip(weights, branch_outs):
        combined = combined + weight[..., None] * branch_out
    return (weights, combined)

def prepare(weight, branch_level, grad_out, alignment):
    level_low = branch_level.astype(jnp.bfloat16)
    level_back = lax.optimization_barrier(level_low).astype(jnp.float32)
    factor = jnp.exp(level_back - branch_level) * weight
    grads_low = (factor[..., None] * grad_out).astype(jnp.bfloat16)
    corr_low = (factor * alignment).astype(jnp.bfloat16)
    corr_back = lax.optimization_barrier(corr_low).astype(jnp.float32)
    return (level_low, level_back, grads_low, corr_low, corr_back)

def reference(query_rows, key_rows, value_rows, out_grad):
    token_count = query_rows.shape[0]
    head_count = HEADS
    head_size = HEAD_DIM
    scaling = float(head_size) ** (-0.5)
    shape_three = (token_count, head_count, head_size)
    queries = query_rows.reshape(shape_three)
    keys_all = key_rows.reshape(shape_three)
    values_all = value_rows.reshape(shape_three)
    plan = ((SEG_A, 1, np.zeros(head_count, dtype=np.int32)), (SEG_B, 8, np.arange(head_count) % 8), (token_count, 64, np.arange(head_count) % 64))
    positions = jnp.arange(token_count, dtype=jnp.int32)[:, None]
    head_ids = jnp.arange(head_count, dtype=jnp.int32)[None, :]
    levels, branch_outs, masks, pieces = ([], [], [], [])
    for seg_len, stride, offsets in plan:

        def segments(source):
            chosen = pick_rows(source, stride, offsets)
            return chosen.reshape((token_count // seg_len, seg_len // stride) + chosen.shape[1:])
        seg_queries = segments(queries)
        seg_keys = segments(keys_all)
        seg_values = segments(values_all)

        def forward_one(triple):
            return attend(triple[0], triple[1], triple[2], scaling)
        seg_levels, seg_outs = lax.map(forward_one, (seg_queries, seg_keys, seg_values))
        levels.append(spread_rows(seg_levels.reshape((-1, head_count)), stride, offsets))
        branch_outs.append(spread_rows(seg_outs.reshape((-1, head_count, head_size)), stride, offsets))
        masks.append(positions % stride == head_ids % stride)
        pieces.append((seg_queries, seg_keys, seg_values))
    weights, combined = combine(levels, branch_outs, masks)
    attended = combined.astype(jnp.bfloat16).reshape(token_count, -1)
    grad_out = out_grad.reshape(shape_three).astype(jnp.float32)
    alignment = lax.optimization_barrier(jnp.sum(grad_out * combined, axis=2))
    total_q = jnp.zeros(shape_three, jnp.float32)
    total_k = jnp.zeros(shape_three, jnp.float32)
    total_v = jnp.zeros(shape_three, jnp.float32)
    for branch_index in range(3):
        seg_len, stride, offsets = plan[branch_index]
        prepared = prepare(pick_rows(weights[branch_index], stride, offsets), pick_rows(levels[branch_index], stride, offsets), pick_rows(grad_out, stride, offsets), pick_rows(alignment, stride, offsets))
        level_back, grads_low, corr_back = (prepared[1], prepared[2], prepared[4])
        seg_queries, seg_keys, seg_values = pieces[branch_index]
        seg_count = seg_queries.shape[0]

        def regroup(source):
            return source.reshape((seg_count, -1) + source.shape[1:])

        def backward_one(group):
            q_part, k_part, v_part, g_part, c_part, l_part = group
            dq_part = query_grads(q_part, k_part, v_part, g_part, c_part, l_part, scaling)
            dk_part, dv_part = key_grads(k_part, v_part, q_part, g_part, c_part, l_part, scaling)
            return (dq_part, dk_part, dv_part)
        dq_seg, dk_seg, dv_seg = lax.map(backward_one, (seg_queries, seg_keys, seg_values, regroup(grads_low), regroup(corr_back), regroup(level_back)))
        total_q = total_q + spread_rows(dq_seg.reshape((-1, head_count, head_size)), stride, offsets)
        total_k = total_k + spread_rows(dk_seg.reshape((-1, head_count, head_size)), stride, offsets)
        total_v = total_v + spread_rows(dv_seg.reshape((-1, head_count, head_size)), stride, offsets)
    d_query = total_q.astype(jnp.bfloat16).reshape(token_count, -1)
    d_key = total_k.astype(jnp.bfloat16).reshape(token_count, -1)
    d_value = total_v.astype(jnp.bfloat16).reshape(token_count, -1)
    return (attended, d_query, d_key, d_value)
```

```python
import functools

import jax
import jax.numpy as jnp
from jax import lax
from jax.experimental import pallas as pl
from jax.experimental.pallas import tpu as pltpu
from jax.sharding import PartitionSpec as P

HEADS = 6
D = 64
SCALE = float(D) ** (-0.5)
AXES = ("outer", "inner")
TEAM = 8
NONE = -1e30
F32 = jnp.float32
BF16 = jnp.bfloat16
VMEM = pl.BlockSpec(memory_space=pltpu.VMEM)


def dot(a, b):
    return jnp.dot(a, b, preferred_element_type=F32)


def dot_t(a, b):
    return lax.dot_general(a, b, (((1,), (1,)), ((), ())), preferred_element_type=F32)


def place():
    member = lax.rem(lax.axis_index("inner"), TEAM)
    return lax.div(member, 2), lax.rem(member, 2)


def head_at(chip, column):
    return 3 * column + jnp.clip(chip - column, 0, 2)


def owns(member):
    return 0 <= member // 2 - member % 2 <= 2


def move(value, mask, keep=lambda source, target: True):
    count = lax.axis_size("outer") * lax.axis_size("inner")
    pairs = [(s, s ^ mask) for s in range(count) if keep(s % TEAM, (s ^ mask) % TEAM)]
    return lax.ppermute(value, AXES, pairs)


def call(body, outs, *args, scratch=()):
    return pl.pallas_call(
        body,
        out_shape=[jax.ShapeDtypeStruct(shape, dtype) for shape, dtype in outs],
        in_specs=[VMEM] * len(args),
        out_specs=[VMEM] * len(outs),
        scratch_shapes=list(scratch),
        compiler_params=pltpu.CompilerParams(vmem_limit_bytes=48 * 2**20),
    )(*args)


def pack_body(q_ref, k_ref, v_ref, g_ref, keep_ref, send_ref, heads_ref):
    chip, column = place()
    q = (q_ref[...].astype(F32) * SCALE).astype(BF16)
    k, v, g = k_ref[...], v_ref[...], g_ref[...]
    for h in range(HEADS):
        cols = slice(h * D, (h + 1) * D)
        heads_ref[h] = jnp.concatenate([k[:, cols], v[:, cols], q[:, cols], g[:, cols]], axis=1)
    for t in range(4):
        keep_ref[t] = heads_ref[head_at(chip ^ t, column)]
        send_ref[t] = heads_ref[head_at(chip ^ t, 1 - column)]


def regroup_body(keep_ref, recv_ref, s1, s2, s3, b_ref, c_ref, wide, thin):
    chip, column = place()
    rows = keep_ref.shape[1]
    picked = 2 * rows // 8
    thin[...] = jnp.zeros_like(thin)
    for t in range(4):
        if t:
            (s1, s2, s3)[t - 1][:rows] = keep_ref[t]
            (s1, s2, s3)[t - 1][rows:] = recv_ref[t]
        wide[:rows] = keep_ref[t, :, : 2 * D].astype(F32)
        wide[rows:] = recv_ref[t, :, : 2 * D].astype(F32)
        chosen = wide[pl.ds(head_at(chip ^ t, column), picked, stride=8), :]
        b_ref[t] = chosen.astype(BF16)
        thin[:picked] = chosen
        c_ref[t] = thin[pl.ds(0, 8, stride=8), :].astype(BF16)


def gather_body(near, far, *refs):
    outs = refs[near + far :]
    for t in range(4):
        at = 0
        for ref in refs[: near + far]:
            size = ref.shape[1]
            outs[t][at : at + size] = ref[t]
            at += size


def main_body(
    near,
    far,
    keep_ref,
    recv_ref,
    r1,
    r2,
    r3,
    n0,
    n1,
    n2,
    n3,
    o0,
    o1,
    o2,
    o3,
    *rest,
):
    near_refs, far_refs = rest[:near], rest[near : near + far]
    (xa, xb, keys, vals, qs, gs, kvt, st, pt, dt, oq, dkv, z1, z2, stats) = rest[near + far :]
    chip, column = place()
    head = head_at(chip, column)
    rows = keep_ref.shape[1]
    total = TEAM * rows
    picked = total // 8
    own_b = pl.ds(head, picked, stride=8)

    blocks = [keep_ref[0], recv_ref[0]]
    for ref in (r1, r2, r3):
        blocks += [ref[:rows], ref[rows:]]
    for i, block in enumerate(blocks):
        at = slice(i * rows, (i + 1) * rows)
        keys[at] = block[:, :D]
        vals[at] = block[:, D : 2 * D]
        qs[at] = block[:, 2 * D : 3 * D]
        gs[at] = block[:, 3 * D :]
        xa[at] = block[:, : 2 * D].astype(F32)
        xb[at] = block[:, 2 * D :].astype(F32)
    kvt[...] = xa[...].T.astype(BF16)

    mine = xb[own_b, :].astype(BF16)
    other = jnp.concatenate([xa[own_b, :].astype(BF16), n0[...], n1[...], n2[...], n3[...]], axis=0)
    kext, vext = other[:, :D], other[:, D:]
    q_b, g_b = mine[:, :D], mine[:, D:]
    extent = other.shape[0]
    chip_b = picked // 4
    span = near * chip_b + 8 * far
    row = lax.broadcasted_iota(jnp.int32, (extent, 1), 0)
    offset = lax.rem(jnp.maximum(row - picked, 0), span)
    inside = (row < picked) | (offset < near * chip_b)
    use_b = inside
    use_c = (inside & (lax.rem(jnp.where(row < picked, row, offset), 8) == 0)) | (
        (~inside) & (lax.rem(jnp.maximum(offset - near * chip_b, 0), 8) < chip_b // 8)
    )
    scores = dot_t(kext, q_b)

    def branch(use):
        masked = jnp.where(use, scores, NONE)
        highest = jnp.max(masked, axis=0, keepdims=True)
        level = highest + jnp.log(jnp.sum(jnp.exp(masked - highest), axis=0, keepdims=True))
        probs = jnp.exp(masked - level).astype(BF16)
        return level, masked, probs

    level_b, masked_b, probs_b = branch(use_b)
    level_c, masked_c, probs_c = branch(use_c)
    vext_t = vext.astype(F32).T.astype(BF16)
    kext_t = kext.astype(F32).T.astype(BF16)
    part_b = dot(vext_t, probs_b)
    part_c = dot(vext_t, probs_c)
    lane = lax.broadcasted_iota(jnp.int32, (1, picked), 1)
    in_c = lax.rem(lane, 8) == 0
    part_c = jnp.where(in_c, part_c, 0.0)
    z1[...] = jnp.zeros_like(z1)
    z2[...] = jnp.full_like(z2, NONE)
    z1[own_b, :] = jnp.concatenate([part_b, part_c], axis=0).T
    level_rows = jnp.concatenate(
        [level_b, jnp.where(in_c, level_c, NONE), jnp.zeros((126, picked), F32)], axis=0
    )
    z2[own_b, :] = level_rows.T

    tile = 256
    chunk = 256
    dkv[...] = jnp.zeros_like(dkv)

    def fold(x, op):
        return op(x.reshape(-1, 8, x.shape[1]), axis=0)

    def one_tile(t, carry):
        here = pl.ds(pl.multiple_of(t * tile, tile), tile)
        q_t, g_t = qs[here, :], gs[here, :]
        top = jnp.full((8, tile), NONE, F32)
        for at in range(0, total, chunk):
            s = dot_t(keys[at : at + chunk, :], q_t)
            st[at : at + chunk, :] = s
            top = jnp.maximum(top, fold(s, jnp.max))
        top = jnp.max(top, axis=0, keepdims=True)
        mass = jnp.zeros((8, tile), F32)
        for at in range(0, total, chunk):
            e = jnp.exp(st[at : at + chunk, :] - top)
            st[at : at + chunk, :] = e
            mass = mass + fold(e, jnp.sum)
        mass = jnp.sum(mass, axis=0, keepdims=True)
        level = top + jnp.log(mass)
        norm = 1.0 / mass
        for at in range(0, total, chunk):
            pt[at : at + chunk, :] = (st[at : at + chunk, :] * norm).astype(BF16)
        part = dot(kvt[D:, :], pt[...])
        rows_a = jnp.concatenate([part, jnp.broadcast_to(level, (D, tile))], axis=0).T
        part_a, level_a = rows_a[:, :D], rows_a[:, D : D + 1]
        others, levels = z1[here, :], z2[here, :]
        lb, lc = levels[:, 0:1], levels[:, 1:2]
        highest = jnp.maximum(jnp.maximum(level_a, lb), lc)
        overall = highest + jnp.log(
            jnp.exp(level_a - highest) + jnp.exp(lb - highest) + jnp.exp(lc - highest)
        )
        w_a, w_b, w_c = jnp.exp(level_a - overall), jnp.exp(lb - overall), jnp.exp(lc - overall)
        combined = w_a * part_a + w_b * others[:, :D] + w_c * others[:, D:]
        g32 = g_t.astype(F32)
        align = jnp.sum(g32 * combined, axis=1, keepdims=True)
        low = level_a.astype(BF16).astype(F32)
        factor = jnp.exp(low - level_a) * w_a
        grads = (factor * g32).astype(BF16)
        corr = (factor * align).astype(BF16).astype(F32)
        column_id = lax.broadcasted_iota(jnp.int32, (tile, 2 * D), 1)
        stats[here, :] = jnp.where(column_id == 0, align, jnp.where(column_id == 1, w_b, w_c))
        across = jnp.where(column_id == 0, corr, low).T
        corr_t, low_t = across[0:1], across[1:2]
        lift = jnp.exp(top - low_t)
        for at in range(0, total, chunk):
            redo = st[at : at + chunk, :] * lift
            dprob = dot_t(vals[at : at + chunk, :], grads)
            dt[at : at + chunk, :tile] = (redo * (dprob - corr_t)).astype(BF16)
            dt[at : at + chunk, tile:] = redo.astype(BF16)
        dq = dot(kvt[:D, :], dt[:, :tile]) * SCALE
        oq[here, :] = jnp.concatenate([combined, dq.T], axis=1)
        zero = jnp.zeros((tile, D), BF16)
        right = jnp.concatenate(
            [jnp.concatenate([q_t, zero], axis=1), jnp.concatenate([zero, grads], axis=1)], axis=0
        )
        for at in range(0, total, chunk):
            dkv[at : at + chunk, :] += dot(dt[at : at + chunk, :], right)
        return carry

    lax.fori_loop(0, total // tile, one_tile, 0)

    numbers = stats[own_b, :]
    align, w_b, w_c = numbers[:, 0:1], numbers[:, 1:2], numbers[:, 2:3]
    g32 = g_b.astype(F32)
    levels_t = jnp.concatenate(
        [level_b, level_c, jnp.zeros((126, picked), F32)], axis=0
    ).T
    dk = jnp.zeros((extent, D), F32)
    dv = jnp.zeros((extent, D), F32)
    dq = jnp.zeros((D, picked), F32)
    for level, weight, masked in (
        (levels_t[:, 0:1], w_b, masked_b),
        (levels_t[:, 1:2], w_c, masked_c),
    ):
        low = level.astype(BF16).astype(F32)
        factor = jnp.exp(low - level) * weight
        grads = (factor * g32).astype(BF16)
        corr = (factor * align).astype(BF16).astype(F32)
        column_id = lax.broadcasted_iota(jnp.int32, (picked, 2 * D), 1)
        across = jnp.where(column_id == 0, corr, low).T
        redo = jnp.exp(masked - across[1:2])
        dscore = (redo * (dot_t(vext, grads) - across[0:1])).astype(BF16)
        dk = dk + dot(dscore, q_b)
        dv = dv + dot(redo.astype(BF16), grads)
        dq = dq + dot(kext_t, dscore)
    both = jnp.concatenate([dk, dv], axis=1)
    dkv[own_b, :] = dkv[own_b, :] + both[:picked]
    oq[own_b, :] = oq[own_b, :] + jnp.concatenate([jnp.zeros_like(dq), dq * SCALE], axis=0).T
    for t in range(4):
        at = picked + t * span
        for ref in near_refs:
            ref[t] = both[at : at + chip_b].astype(BF16)
            at += chip_b
        for ref in far_refs:
            ref[t] = both[at : at + 8].astype(BF16)
            at += 8
    for t, ref in enumerate((o0, o1, o2, o3)):
        at = slice(2 * t * rows, 2 * (t + 1) * rows)
        ref[:, : 2 * D] = dkv[at, :].astype(BF16)
        ref[:, 2 * D :] = oq[at, :].astype(BF16)


def sum_body(near, far, *refs):
    outs, thin = refs[near + far : -1], refs[-1]
    picked = refs[0].shape[1]
    for t in range(4):
        thin[...] = jnp.zeros_like(thin)
        for ref in refs[:near]:
            thin[:picked] += ref[t].astype(F32)
        every = pl.ds(0, 8, stride=8)
        for ref in refs[near : near + far]:
            thin[every, :] = thin[every, :] + ref[t].astype(F32)
        outs[t][...] = thin[:picked].astype(BF16)


def middle_body(m0, m1, m2, m3, t0, t1, t2, t3, keep_ref, send_ref, wide):
    chip, column = place()
    rows = keep_ref.shape[1]
    for t, (main, extra) in enumerate(((m0, t0), (m1, t1), (m2, t2), (m3, t3))):
        wide[...] = main[:, : 2 * D].astype(F32)
        chosen = pl.ds(head_at(chip ^ t, column), extra.shape[0], stride=8)
        wide[chosen, :] = wide[chosen, :] + extra[...].astype(F32)
        keep_ref[t, :, : 2 * D] = wide[:rows].astype(BF16)
        send_ref[t, :, : 2 * D] = wide[rows:].astype(BF16)
        keep_ref[t, :, 2 * D :] = main[:rows, 2 * D :]
        send_ref[t, :, 2 * D :] = main[rows:, 2 * D :]


def unpack_body(keep_ref, recv_ref, out_ref, dq_ref, dk_ref, dv_ref, heads_ref):
    chip, column = place()
    for side in range(2):

        @pl.when(column == side)
        def _():
            for h in range(HEADS):
                source = keep_ref if h // 3 == side else recv_ref
                heads_ref[h] = source[(h % 3 + h // 3) ^ chip]

    for at, ref in ((0, dk_ref), (1, dv_ref), (2, out_ref), (3, dq_ref)):
        ref[...] = jnp.concatenate(
            [heads_ref[h, :, at * D : (at + 1) * D] for h in range(HEADS)], axis=1
        )


def shards(query_rows, key_rows, value_rows, out_grad):
    rows = query_rows.shape[0]
    width = 4 * D
    teams = lax.axis_size("outer") * lax.axis_size("inner") // TEAM
    near = 2 * lax.axis_size("inner") // TEAM - 1
    far = teams - 1 - near
    to_owner = lambda source, target: owns(target)
    from_owner = lambda source, target: owns(source)
    both_own = lambda source, target: owns(source)
    total = TEAM * rows
    chip_b = 2 * rows // 8
    span = near * chip_b + 8 * far

    block = ((4, rows, width), BF16)
    keep, send = call(
        pack_body, [block, block], query_rows, key_rows, value_rows, out_grad,
        scratch=[pltpu.VMEM((HEADS, rows, width), BF16)],
    )
    recv = move(send, 1)
    s1, s2, s3, picked_b, picked_c = call(
        regroup_body,
        [((2 * rows, width), BF16)] * 3 + [((4, chip_b, 2 * D), BF16), ((4, 8, 2 * D), BF16)],
        keep,
        recv,
        scratch=[pltpu.VMEM((2 * rows, 2 * D), F32), pltpu.VMEM((64, 2 * D), F32)],
    )
    from_near = [move(picked_b, TEAM * j) for j in range(1, near + 1)]
    from_far = [move(picked_c, TEAM * j) for j in range(near + 1, teams)]
    got = [move(s, 2 * t, to_owner) for t, s in ((1, s1), (2, s2), (3, s3))]
    nears = call(
        functools.partial(gather_body, near, far),
        [((span, 2 * D), BF16)] * 4,
        *from_near,
        *from_far,
    )
    nears = [nears[0]] + [move(nears[t], 2 * t, to_owner) for t in (1, 2, 3)]
    results = call(
        functools.partial(main_body, near, far),
        [((2 * rows, width), BF16)] * 4
        + [((4, chip_b, 2 * D), BF16)] * near
        + [((4, 8, 2 * D), BF16)] * far,
        keep,
        recv,
        *got,
        *nears,
        scratch=[
            pltpu.VMEM((total, 2 * D), F32),
            pltpu.VMEM((total, 2 * D), F32),
            pltpu.VMEM((total, D), BF16),
            pltpu.VMEM((total, D), BF16),
            pltpu.VMEM((total, D), BF16),
            pltpu.VMEM((total, D), BF16),
            pltpu.VMEM((2 * D, total), BF16),
            pltpu.VMEM((total, 256), F32),
            pltpu.VMEM((total, 256), BF16),
            pltpu.VMEM((total, 512), BF16),
            pltpu.VMEM((total, 2 * D), F32),
            pltpu.VMEM((total, 2 * D), F32),
            pltpu.VMEM((total, 2 * D), F32),
            pltpu.VMEM((total, 2 * D), F32),
            pltpu.VMEM((total, 2 * D), F32),
        ],
    )
    mains, near_parts, far_parts = results[:4], results[4 : 4 + near], results[4 + near :]
    near_parts = [move(x, TEAM * j, both_own) for j, x in enumerate(near_parts, 1)]
    far_parts = [move(x, TEAM * j, both_own) for j, x in enumerate(far_parts, near + 1)]
    back = [mains[0]] + [move(mains[t], 2 * t, from_owner) for t in (1, 2, 3)]
    sums = call(
        functools.partial(sum_body, near, far),
        [((chip_b, 2 * D), BF16)] * 4,
        *near_parts,
        *far_parts,
        scratch=[pltpu.VMEM((64, 2 * D), F32)],
    )
    sums = [sums[0]] + [move(sums[t], 2 * t, from_owner) for t in (1, 2, 3)]
    keep, send = call(
        middle_body, [block, block], *back, *sums,
        scratch=[pltpu.VMEM((2 * rows, 2 * D), F32)],
    )
    recv = move(send, 1)
    out = ((rows, HEADS * D), BF16)
    return tuple(
        call(
            unpack_body, [out] * 4, keep, recv,
            scratch=[pltpu.VMEM((HEADS, rows, width), BF16)],
        )
    )


def solution(mesh):
    spec = P(AXES, None)
    return jax.shard_map(
        shards, mesh=mesh, in_specs=(spec,) * 4, out_specs=(spec,) * 4, check_vma=False
    )
```

```python
import functools

import jax
import jax.numpy as jnp
from jax import lax
from jax.experimental import pallas as pl
from jax.experimental.pallas import tpu as pltpu
from jax.sharding import PartitionSpec as P

HEADS = 6
D = 64
SCALE = float(D) ** (-0.5)
AXES = ("outer", "inner")
TEAM = 8
NONE = -1e30
F32 = jnp.float32
BF16 = jnp.bfloat16
VMEM = pl.BlockSpec(memory_space=pltpu.VMEM)
HBM = pl.BlockSpec(memory_space=pltpu.HBM)


def dot(a, b):
    return jnp.dot(a, b, preferred_element_type=F32)


def dot_t(a, b):
    return lax.dot_general(a, b, (((1,), (1,)), ((), ())), preferred_element_type=F32)


def place():
    member = lax.rem(lax.axis_index("inner"), TEAM)
    return lax.div(member, 2), lax.rem(member, 2)


def head_at(chip, column):
    return 3 * column + jnp.clip(chip - column, 0, 2)


def owns(member):
    return 0 <= member // 2 - member % 2 <= 2


def move(value, mask, keep=lambda source, target: True):
    count = lax.axis_size("outer") * lax.axis_size("inner")
    pairs = [(s, s ^ mask) for s in range(count) if keep(s % TEAM, (s ^ mask) % TEAM)]
    return lax.ppermute(value, AXES, pairs)


def call(body, outs, *args, scratch=(), specs=None):
    return pl.pallas_call(
        body,
        out_shape=[jax.ShapeDtypeStruct(shape, dtype) for shape, dtype in outs],
        in_specs=specs or [VMEM] * len(args),
        out_specs=[VMEM] * len(outs),
        scratch_shapes=list(scratch),
        compiler_params=pltpu.CompilerParams(vmem_limit_bytes=48 * 2**20),
    )(*args)


def side_by_side(x):
    return jnp.concatenate([x[at : at + 8] for at in range(0, x.shape[0], 8)], axis=1)


def pack_body(
    near,
    q_hbm,
    k_hbm,
    v_hbm,
    g_hbm,
    keep_ref,
    send_ref,
    slots_ref,
    heads_ref,
    q_ref,
    k_ref,
    v_ref,
    g_ref,
    wide,
    thin,
    picks,
    sems,
):
    copies = [
        pltpu.make_async_copy(source, target, sems.at[i])
        for i, (source, target) in enumerate(
            ((k_hbm, k_ref), (v_hbm, v_ref), (q_hbm, q_ref), (g_hbm, g_ref))
        )
    ]
    for copy in copies:
        copy.start()
    for copy in copies:
        copy.wait()
    chip, column = place()
    q = (q_ref[...].astype(F32) * SCALE).astype(BF16)
    k, v, g = k_ref[...], v_ref[...], g_ref[...]
    picked = k.shape[0] // 8
    thin[...] = jnp.zeros_like(thin)
    for h in range(HEADS):
        cols = slice(h * D, (h + 1) * D)
        pair = jnp.concatenate([k[:, cols], v[:, cols]], axis=1)
        heads_ref[h, :, : 2 * D] = pair
        heads_ref[h, :, 2 * D :] = jnp.concatenate([q[:, cols], g[:, cols]], axis=1)
        wide[...] = pair.astype(F32)
        chosen = wide[pl.ds(h, picked, stride=8), :]
        picks[0, h] = side_by_side(chosen).astype(BF16)
        thin[:picked] = chosen
        few = thin[pl.ds(0, 8, stride=8), :]
        picks[1, h] = side_by_side(
            jnp.concatenate([few, jnp.zeros((picked - 8, 2 * D), F32)], axis=0)
        ).astype(BF16)
    for t in range(4):
        keep_ref[t] = heads_ref[head_at(chip ^ t, column)]
        send_ref[t] = heads_ref[head_at(chip ^ t, 1 - column)]
    segment = lax.div(my_team(), near + 1)
    for team in range(slots_ref.shape[0] // TEAM):
        other = (segment != team // (near + 1)).astype(jnp.int32)
        for member in range(TEAM):
            head = 3 * (member % 2) + min(max(member // 2 - member % 2, 0), 2)
            slots_ref[team * TEAM + member] = picks[other, head]


def my_team():
    teams_in = lax.axis_size("inner") // TEAM
    return lax.axis_index("outer") * teams_in + lax.div(lax.axis_index("inner"), TEAM)


def regroup_body(keep_ref, recv_ref, s1, s2, s3):
    rows = keep_ref.shape[1]
    for t, ref in enumerate((s1, s2, s3), 1):
        ref[:rows] = keep_ref[t]
        ref[rows:] = recv_ref[t]


def copy_body(value_ref, out_ref):
    out_ref[...] = value_ref[...]


def main_body(
    near,
    far,
    keep_ref,
    recv_ref,
    r1,
    r2,
    r3,
    slots_ref,
    o0,
    o1,
    o2,
    o3,
    parts_ref,
    *scratch,
):
    (xa, xb, keys, vals, qt, gt, kvt, st, oq, dkv, z, zt, stats) = scratch
    chip, column = place()
    head = head_at(chip, column)
    rows = keep_ref.shape[1]
    total = TEAM * rows
    picked = total // 8
    own_b = pl.ds(head, picked, stride=8)

    blocks = [keep_ref[0], recv_ref[0]]
    for ref in (r1, r2, r3):
        blocks += [ref[:rows], ref[rows:]]
    for i, block in enumerate(blocks):
        at = slice(i * rows, (i + 1) * rows)
        keys[at] = block[:, :D]
        vals[at] = block[:, D : 2 * D]
        xa[at] = block[:, : 2 * D].astype(F32)
        xb[at] = block[:, 2 * D :].astype(F32)
    kvt[...] = xa[...].T.astype(BF16)
    flipped = xb[...].T
    qt[...] = flipped[:D].astype(BF16)
    gt[...] = flipped[D:]

    mine = xb[own_b, :].astype(BF16)
    team = my_team()
    pieces = [xa[own_b, :]]
    for j in range(1, near + far + 1):
        slot = pl.ds((team ^ j) * TEAM, TEAM)
        for i in range(rows // 64 if j <= near else 1):
            part = slots_ref[slot, :, i * 2 * D : (i + 1) * 2 * D]
            pieces.append(part.astype(F32).reshape(-1, 2 * D))
    other = jnp.concatenate(pieces, axis=0).astype(BF16)
    kext, vext = other[:, :D], other[:, D:]
    q_b, g_b = mine[:, :D], mine[:, D:]
    extent = other.shape[0]
    row = lax.broadcasted_iota(jnp.int32, (extent, 1), 0)
    use_b = row < (near + 1) * picked
    use_c = lax.rem(row, 8) < jnp.where(use_b, 1, rows // 64)
    scores = dot_t(kext, q_b)

    def branch(use):
        masked = jnp.where(use, scores, NONE)
        highest = jnp.max(masked, axis=0, keepdims=True)
        level = highest + jnp.log(jnp.sum(jnp.exp(masked - highest), axis=0, keepdims=True))
        probs = jnp.exp(masked - level).astype(BF16)
        return level, masked, probs

    level_b, masked_b, probs_b = branch(use_b)
    level_c, masked_c, probs_c = branch(use_c)
    vext_t = vext.astype(F32).T.astype(BF16)
    kext_t = kext.astype(F32).T.astype(BF16)
    part_b = dot(vext_t, probs_b)
    part_c = dot(vext_t, probs_c)
    lane = lax.broadcasted_iota(jnp.int32, (1, picked), 1)
    in_c = lax.rem(lane, 8) == 0
    level_in = jnp.where(in_c, level_c, NONE)
    top = jnp.maximum(level_b, level_in)
    level_bc = top + jnp.log(jnp.exp(level_b - top) + jnp.exp(level_in - top))
    part_bc = jnp.exp(level_b - level_bc) * part_b + jnp.exp(level_in - level_bc) * part_c
    lanes = lax.broadcasted_iota(jnp.int32, z.shape, 1)
    z[...] = jnp.where(lanes < D, 0.0, NONE)
    z[own_b, :] = jnp.concatenate([part_bc, jnp.broadcast_to(level_bc, (D, picked))], axis=0).T
    zt[...] = z[...].T

    tile = total
    chunk = 2 * rows
    dkv[...] = jnp.zeros_like(dkv)
    zero = jnp.zeros((D, tile), BF16)

    def fold(x, op):
        return op(x.reshape(-1, 8, x.shape[1]), axis=0)

    def one_tile(t, carry):
        here = pl.ds(pl.multiple_of(t * tile, tile), tile)
        q_t = qt[:, here]
        top = jnp.full((8, tile), NONE, F32)
        for at in range(0, total, chunk):
            s = dot(keys[at : at + chunk, :], q_t)
            st[at : at + chunk, :] = s
            top = jnp.maximum(top, fold(s, jnp.max))
        top = jnp.max(top, axis=0, keepdims=True)
        mass = jnp.zeros((8, tile), F32)
        for at in range(0, total, chunk):
            e = jnp.exp(st[at : at + chunk, :] - top)
            st[at : at + chunk, :] = e
            mass = mass + fold(e, jnp.sum)
        mass = jnp.sum(mass, axis=0, keepdims=True)
        level = top + jnp.log(mass)
        norm = 1.0 / mass
        part = [jnp.zeros((D, tile), F32)] * 2
        for i, at in enumerate(range(0, total, chunk)):
            probs = (st[at : at + chunk, :] * norm).astype(BF16)
            part[i % 2] = part[i % 2] + dot(kvt[D:, at : at + chunk], probs)
        level_o = zt[D : D + 1, here]
        highest = jnp.maximum(level, level_o)
        overall = highest + jnp.log(jnp.exp(level - highest) + jnp.exp(level_o - highest))
        weight = jnp.exp(level - overall)
        combined = weight * (part[0] + part[1]) + jnp.exp(level_o - overall) * zt[:D, here]
        g_t = gt[:, here]
        align = jnp.sum(g_t * combined, axis=0, keepdims=True)
        low = level.astype(BF16).astype(F32)
        factor = jnp.exp(low - level) * weight
        grads = (factor * g_t).astype(BF16)
        corr = (factor * align).astype(BF16).astype(F32)
        lift = jnp.exp(top - low)
        right = jnp.concatenate(
            [jnp.concatenate([q_t, zero], axis=1), jnp.concatenate([zero, grads], axis=1)], axis=0
        )
        dq = [jnp.zeros((D, tile), F32)] * 2
        for i, at in enumerate(range(0, total, chunk)):
            redo = st[at : at + chunk, :] * lift
            dprob = dot(vals[at : at + chunk, :], grads)
            dscore = (redo * (dprob - corr)).astype(BF16)
            dq[i % 2] = dq[i % 2] + dot(kvt[:D, at : at + chunk], dscore)
            dkv[at : at + chunk, :] += dot_t(
                jnp.concatenate([dscore, redo.astype(BF16)], axis=1), right
            )
        oq[here, :] = jnp.concatenate([combined, (dq[0] + dq[1]) * SCALE], axis=0).T
        stats[here, :] = jnp.concatenate(
            [align, overall, jnp.zeros((126, tile), F32)], axis=0
        ).T
        return carry

    lax.fori_loop(0, total // tile, one_tile, 0)

    numbers = stats[own_b, :]
    align, overall = numbers[:, 0:1], numbers[:, 1:2]
    g32 = g_b.astype(F32)
    levels_t = jnp.concatenate(
        [level_b, level_c, level_in, jnp.zeros((125, picked), F32)], axis=0
    ).T
    dk = jnp.zeros((extent, D), F32)
    dv = jnp.zeros((extent, D), F32)
    dq = jnp.zeros((D, picked), F32)
    for level, weight, masked in (
        (levels_t[:, 0:1], jnp.exp(levels_t[:, 0:1] - overall), masked_b),
        (levels_t[:, 1:2], jnp.exp(levels_t[:, 2:3] - overall), masked_c),
    ):
        low = level.astype(BF16).astype(F32)
        factor = jnp.exp(low - level) * weight
        grads = (factor * g32).astype(BF16)
        corr = (factor * align).astype(BF16).astype(F32)
        column_id = lax.broadcasted_iota(jnp.int32, (picked, 2 * D), 1)
        across = jnp.where(column_id == 0, corr, low).T
        redo = jnp.exp(masked - across[1:2])
        dscore = (redo * (dot_t(vext, grads) - across[0:1])).astype(BF16)
        dk = dk + dot(dscore, q_b)
        dv = dv + dot(redo.astype(BF16), grads)
        dq = dq + dot(kext_t, dscore)
    both = jnp.concatenate([dk, dv], axis=1)
    dkv[own_b, :] = dkv[own_b, :] + both[:picked]
    oq[own_b, :] = oq[own_b, :] + jnp.concatenate([jnp.zeros_like(dq), dq * SCALE], axis=0).T
    parts_ref[...] = jnp.zeros_like(parts_ref)
    at = picked
    for j in range(1, near + far + 1):
        slot = pl.ds((team ^ j) * TEAM, TEAM)
        for i in range(rows // 64 if j <= near else 1):
            piece = both[at : at + 8 * TEAM].reshape(TEAM, 8, 2 * D)
            parts_ref[slot, :, i * 2 * D : (i + 1) * 2 * D] = piece.astype(BF16)
            at += 8 * TEAM
    for t, ref in enumerate((o0, o1, o2, o3)):
        at = slice(2 * t * rows, 2 * (t + 1) * rows)
        ref[:, : 2 * D] = dkv[at, :].astype(BF16)
        ref[:, 2 * D :] = oq[at, :].astype(BF16)


def middle_body(m0, m1, m2, m3, parts_ref, keep_ref, send_ref):
    rows = keep_ref.shape[1]
    for t, main in enumerate((m0, m1, m2, m3)):
        keep_ref[t] = main[:rows]
        send_ref[t] = main[rows:]


def unpack_body(near, keep_ref, recv_ref, parts_ref, out_ref, dq_ref, dk_ref, dv_ref, heads_ref, wide):
    chip, column = place()
    for side in range(2):

        @pl.when(column == side)
        def _():
            for h in range(HEADS):
                source = keep_ref if h // 3 == side else recv_ref
                heads_ref[h] = source[(h % 3 + h // 3) ^ chip]

    rows = keep_ref.shape[1]
    team = my_team()
    teams = parts_ref.shape[0] // TEAM
    for h in range(HEADS):
        member = 2 * (h % 3 + h // 3) + h // 3
        wide[h] = heads_ref[h, :, : 2 * D].astype(F32)
        for j in range(1, teams):
            part = parts_ref[(team ^ j) * TEAM + member].astype(F32)
            pieces = [part[:, i * 2 * D : (i + 1) * 2 * D] for i in range(rows // 64)]
            if j <= near:
                chosen, part = pl.ds(h, rows // 8, stride=8), jnp.concatenate(pieces, axis=0)
            else:
                chosen, part = pl.ds(h, rows // 64, stride=64), pieces[0][: rows // 64]
            wide[h, chosen, :] = wide[h, chosen, :] + part
    for at, ref in ((0, dk_ref), (1, dv_ref)):
        ref[...] = jnp.concatenate(
            [wide[h, :, at * D : (at + 1) * D] for h in range(HEADS)], axis=1
        ).astype(BF16)
    for at, ref in ((2, out_ref), (3, dq_ref)):
        ref[...] = jnp.concatenate(
            [heads_ref[h, :, at * D : (at + 1) * D] for h in range(HEADS)], axis=1
        )


def exchange(slots):
    slots = lax.all_to_all(slots, AXES, 0, 0)
    return slots


def shards(query_rows, key_rows, value_rows, out_grad):
    rows = query_rows.shape[0]
    width = 4 * D
    count = lax.axis_size("outer") * lax.axis_size("inner")
    near = 2 * lax.axis_size("inner") // TEAM - 1
    far = count // TEAM - 1 - near
    to_owner = lambda source, target: owns(target)
    from_owner = lambda source, target: owns(source)
    total = TEAM * rows

    block = ((4, rows, width), BF16)
    slots_shape = ((count, 8, rows // 64 * 2 * D), BF16)
    given = pltpu.VMEM((rows, HEADS * D), BF16)
    keep, send, slots = call(
        functools.partial(pack_body, near),
        [block, block, slots_shape],
        *[pltpu.with_memory_space_constraint(x, pltpu.HBM) for x in (query_rows, key_rows, value_rows, out_grad)],
        scratch=[pltpu.VMEM((HEADS, rows, width), BF16)] + [given] * 4
        + [
            pltpu.VMEM((rows, 2 * D), F32),
            pltpu.VMEM((64, 2 * D), F32),
            pltpu.VMEM((2, HEADS, 8, rows // 64 * 2 * D), BF16),
            pltpu.SemaphoreType.DMA((4,)),
        ],
        specs=[HBM] * 4,
    )
    recv = move(send, 1)
    s1, s2, s3 = call(regroup_body, [((2 * rows, width), BF16)] * 3, keep, recv)
    got = [move(s, 2 * t, to_owner) for t, s in ((1, s1), (2, s2), (3, s3))]
    slots = exchange(slots)
    *mains, parts = call(
        functools.partial(main_body, near, far),
        [((2 * rows, width), BF16)] * 4 + [slots_shape],
        keep,
        recv,
        *got,
        slots,
        scratch=[
            pltpu.VMEM((total, 2 * D), F32),
            pltpu.VMEM((total, 2 * D), F32),
            pltpu.VMEM((total, D), BF16),
            pltpu.VMEM((total, D), BF16),
            pltpu.VMEM((D, total), BF16),
            pltpu.VMEM((D, total), F32),
            pltpu.VMEM((2 * D, total), BF16),
            pltpu.VMEM((total, total), F32),
            pltpu.VMEM((total, 2 * D), F32),
            pltpu.VMEM((total, 2 * D), F32),
            pltpu.VMEM((total, 2 * D), F32),
            pltpu.VMEM((2 * D, total), F32),
            pltpu.VMEM((total, 2 * D), F32),
        ],
    )
    back = [mains[0]] + [move(mains[t], 2 * t, from_owner) for t in (1, 2, 3)]
    parts = exchange(parts)
    keep, send = call(
        middle_body, [block, block], *back, parts, specs=[VMEM] * 4 + [HBM]
    )
    recv = move(send, 1)
    out = ((rows, HEADS * D), BF16)
    return tuple(
        call(
            functools.partial(unpack_body, near), [out] * 4, keep, recv, parts,
            scratch=[
                pltpu.VMEM((HEADS, rows, width), BF16),
                pltpu.VMEM((HEADS, rows, 2 * D), F32),
            ],
        )
    )


def solution(mesh):
    spec = P(AXES, None)
    return jax.shard_map(
        shards, mesh=mesh, in_specs=(spec,) * 4, out_specs=(spec,) * 4, check_vma=False
    )
```

```python
import functools

import jax
import jax.numpy as jnp
from jax import lax
from jax.experimental import pallas as pl
from jax.experimental.pallas import tpu as pltpu
from jax.sharding import PartitionSpec as P

HEADS = 6
D = 64
SCALE = float(D) ** (-0.5)
AXES = ("outer", "inner")
TEAM = 8
NONE = -1e30
F32 = jnp.float32
BF16 = jnp.bfloat16
VMEM = pl.BlockSpec(memory_space=pltpu.VMEM)
HBM = pl.BlockSpec(memory_space=pltpu.HBM)


def dot(a, b):
    return jnp.dot(a, b, preferred_element_type=F32)


def dot_t(a, b):
    return lax.dot_general(a, b, (((1,), (1,)), ((), ())), preferred_element_type=F32)


def place():
    member = lax.rem(lax.axis_index("inner"), TEAM)
    return lax.div(member, 2), lax.rem(member, 2)


def head_at(chip, column):
    return 3 * column + jnp.clip(chip - column, 0, 2)


def owns(member):
    return 0 <= member // 2 - member % 2 <= 2


def move(value, mask, keep=lambda source, target: True):
    count = lax.axis_size("outer") * lax.axis_size("inner")
    pairs = [(s, s ^ mask) for s in range(count) if keep(s % TEAM, (s ^ mask) % TEAM)]
    return lax.ppermute(value, AXES, pairs)


def call(body, outs, *args, scratch=(), specs=None):
    return pl.pallas_call(
        body,
        out_shape=[jax.ShapeDtypeStruct(shape, dtype) for shape, dtype in outs],
        in_specs=specs or [VMEM] * len(args),
        out_specs=[VMEM] * len(outs),
        scratch_shapes=list(scratch),
        compiler_params=pltpu.CompilerParams(vmem_limit_bytes=48 * 2**20),
    )(*args)


def side_by_side(x):
    return jnp.concatenate([x[at : at + 8] for at in range(0, x.shape[0], 8)], axis=1)


def pack_body(
    near,
    q_hbm,
    k_hbm,
    v_hbm,
    g_hbm,
    keep_ref,
    send_ref,
    slots_ref,
    heads_ref,
    q_ref,
    k_ref,
    v_ref,
    g_ref,
    wide,
    thin,
    picks,
    sems,
):
    copies = [
        pltpu.make_async_copy(source, target, sems.at[i])
        for i, (source, target) in enumerate(
            ((k_hbm, k_ref), (v_hbm, v_ref), (q_hbm, q_ref), (g_hbm, g_ref))
        )
    ]
    for copy in copies:
        copy.start()
    for copy in copies:
        copy.wait()
    chip, column = place()
    q = (q_ref[...].astype(F32) * SCALE).astype(BF16)
    k, v, g = k_ref[...], v_ref[...], g_ref[...]
    picked = k.shape[0] // 8
    thin[...] = jnp.zeros_like(thin)
    for h in range(HEADS):
        cols = slice(h * D, (h + 1) * D)
        pair = jnp.concatenate([k[:, cols], v[:, cols]], axis=1)
        heads_ref[h, :, : 2 * D] = pair
        heads_ref[h, :, 2 * D :] = jnp.concatenate([q[:, cols], g[:, cols]], axis=1)
        wide[...] = pair.astype(F32)
        chosen = wide[pl.ds(h, picked, stride=8), :]
        picks[0, h] = side_by_side(chosen).astype(BF16)
        thin[:picked] = chosen
        few = thin[pl.ds(0, 8, stride=8), :]
        picks[1, h] = side_by_side(
            jnp.concatenate([few, jnp.zeros((picked - 8, 2 * D), F32)], axis=0)
        ).astype(BF16)
    for t in range(4):
        keep_ref[t] = heads_ref[head_at(chip ^ t, column)]
        send_ref[t] = heads_ref[head_at(chip ^ t, 1 - column)]
    segment = lax.div(my_team(), near + 1)
    for team in range(slots_ref.shape[0] // TEAM):
        other = (segment != team // (near + 1)).astype(jnp.int32)
        for member in range(TEAM):
            head = 3 * (member % 2) + min(max(member // 2 - member % 2, 0), 2)
            slots_ref[team * TEAM + member] = picks[other, head]


def my_team():
    teams_in = lax.axis_size("inner") // TEAM
    return lax.axis_index("outer") * teams_in + lax.div(lax.axis_index("inner"), TEAM)


def regroup_body(keep_ref, recv_ref, s1, s2, s3):
    rows = keep_ref.shape[1]
    for t, ref in enumerate((s1, s2, s3), 1):
        ref[:rows] = keep_ref[t]
        ref[rows:] = recv_ref[t]


def copy_body(value_ref, out_ref):
    out_ref[...] = value_ref[...]


def main_body(
    near,
    far,
    keep_ref,
    recv_ref,
    r2,
    r3,
    r1,
    slots_ref,
    o0,
    o1,
    o2,
    o3,
    parts_ref,
    *scratch,
):
    (xa, xb, keys, vals, qt, gt, kvt, st, oq, dkv, z, zt, stats) = scratch
    chip, column = place()
    head = head_at(chip, column)
    rows = keep_ref.shape[1]
    total = TEAM * rows
    picked = total // 8
    own_b = pl.ds(head, picked, stride=8)

    blocks = [keep_ref[0], recv_ref[0]]
    for ref in (r1, r2, r3):
        blocks += [ref[:rows], ref[rows:]]
    for i, block in enumerate(blocks):
        at = slice(i * rows, (i + 1) * rows)
        keys[at] = block[:, :D]
        vals[at] = block[:, D : 2 * D]
        xa[at] = block[:, : 2 * D].astype(F32)
        xb[at] = block[:, 2 * D :].astype(F32)
    kvt[...] = xa[...].T.astype(BF16)
    flipped = xb[...].T
    qt[...] = flipped[:D].astype(BF16)
    gt[...] = flipped[D:]

    mine = xb[own_b, :].astype(BF16)
    team = my_team()
    pieces = [xa[own_b, :]]
    for j in range(1, near + far + 1):
        slot = pl.ds((team ^ j) * TEAM, TEAM)
        for i in range(rows // 64 if j <= near else 1):
            part = slots_ref[slot, :, i * 2 * D : (i + 1) * 2 * D]
            pieces.append(part.astype(F32).reshape(-1, 2 * D))
    other = jnp.concatenate(pieces, axis=0).astype(BF16)
    kext, vext = other[:, :D], other[:, D:]
    q_b, g_b = mine[:, :D], mine[:, D:]
    extent = other.shape[0]
    row = lax.broadcasted_iota(jnp.int32, (extent, 1), 0)
    use_b = row < (near + 1) * picked
    use_c = lax.rem(row, 8) < jnp.where(use_b, 1, rows // 64)
    scores = dot_t(kext, q_b)

    def branch(use):
        masked = jnp.where(use, scores, NONE)
        highest = jnp.max(masked, axis=0, keepdims=True)
        level = highest + jnp.log(jnp.sum(jnp.exp(masked - highest), axis=0, keepdims=True))
        probs = jnp.exp(masked - level).astype(BF16)
        return level, masked, probs

    level_b, masked_b, probs_b = branch(use_b)
    level_c, masked_c, probs_c = branch(use_c)
    vext_t = vext.astype(F32).T.astype(BF16)
    kext_t = kext.astype(F32).T.astype(BF16)
    part_b = dot(vext_t, probs_b)
    part_c = dot(vext_t, probs_c)
    lane = lax.broadcasted_iota(jnp.int32, (1, picked), 1)
    in_c = lax.rem(lane, 8) == 0
    level_in = jnp.where(in_c, level_c, NONE)
    top = jnp.maximum(level_b, level_in)
    level_bc = top + jnp.log(jnp.exp(level_b - top) + jnp.exp(level_in - top))
    part_bc = jnp.exp(level_b - level_bc) * part_b + jnp.exp(level_in - level_bc) * part_c
    lanes = lax.broadcasted_iota(jnp.int32, z.shape, 1)
    z[...] = jnp.where(lanes < D, 0.0, NONE)
    z[own_b, :] = jnp.concatenate([part_bc, jnp.broadcast_to(level_bc, (D, picked))], axis=0).T
    zt[...] = z[...].T

    tile = total
    chunk = 2 * rows
    dkv[...] = jnp.zeros_like(dkv)
    zero = jnp.zeros((D, tile), BF16)

    def fold(x, op):
        return op(x.reshape(-1, 8, x.shape[1]), axis=0)

    def one_tile(t, carry):
        here = pl.ds(pl.multiple_of(t * tile, tile), tile)
        q_t = qt[:, here]
        top = jnp.full((8, tile), NONE, F32)
        for at in range(0, total, chunk):
            s = dot(keys[at : at + chunk, :], q_t)
            st[at : at + chunk, :] = s
            top = jnp.maximum(top, fold(s, jnp.max))
        top = jnp.max(top, axis=0, keepdims=True)
        mass = jnp.zeros((8, tile), F32)
        for at in range(0, total, chunk):
            e = jnp.exp(st[at : at + chunk, :] - top)
            st[at : at + chunk, :] = e
            mass = mass + fold(e, jnp.sum)
        mass = jnp.sum(mass, axis=0, keepdims=True)
        level = top + jnp.log(mass)
        norm = 1.0 / mass
        part = [jnp.zeros((D, tile), F32)] * 2
        for i, at in enumerate(range(0, total, chunk)):
            probs = (st[at : at + chunk, :] * norm).astype(BF16)
            part[i % 2] = part[i % 2] + dot(kvt[D:, at : at + chunk], probs)
        level_o = zt[D : D + 1, here]
        highest = jnp.maximum(level, level_o)
        overall = highest + jnp.log(jnp.exp(level - highest) + jnp.exp(level_o - highest))
        weight = jnp.exp(level - overall)
        combined = weight * (part[0] + part[1]) + jnp.exp(level_o - overall) * zt[:D, here]
        g_t = gt[:, here]
        align = jnp.sum(g_t * combined, axis=0, keepdims=True)
        low = level.astype(BF16).astype(F32)
        factor = jnp.exp(low - level) * weight
        grads = (factor * g_t).astype(BF16)
        corr = (factor * align).astype(BF16).astype(F32)
        lift = jnp.exp(top - low)
        right = jnp.concatenate(
            [jnp.concatenate([q_t, zero], axis=1), jnp.concatenate([zero, grads], axis=1)], axis=0
        )
        dq = [jnp.zeros((D, tile), F32)] * 2
        for i, at in enumerate(range(0, total, chunk)):
            redo = st[at : at + chunk, :] * lift
            dprob = dot(vals[at : at + chunk, :], grads)
            dscore = (redo * (dprob - corr)).astype(BF16)
            dq[i % 2] = dq[i % 2] + dot(kvt[:D, at : at + chunk], dscore)
            dkv[at : at + chunk, :] += dot_t(
                jnp.concatenate([dscore, redo.astype(BF16)], axis=1), right
            )
        oq[here, :] = jnp.concatenate([combined, (dq[0] + dq[1]) * SCALE], axis=0).T
        stats[here, :] = jnp.concatenate(
            [align, overall, jnp.zeros((126, tile), F32)], axis=0
        ).T
        return carry

    lax.fori_loop(0, total // tile, one_tile, 0)

    numbers = stats[own_b, :]
    align, overall = numbers[:, 0:1], numbers[:, 1:2]
    g32 = g_b.astype(F32)
    levels_t = jnp.concatenate(
        [level_b, level_c, level_in, jnp.zeros((125, picked), F32)], axis=0
    ).T
    dk = jnp.zeros((extent, D), F32)
    dv = jnp.zeros((extent, D), F32)
    dq = jnp.zeros((D, picked), F32)
    for level, weight, masked in (
        (levels_t[:, 0:1], jnp.exp(levels_t[:, 0:1] - overall), masked_b),
        (levels_t[:, 1:2], jnp.exp(levels_t[:, 2:3] - overall), masked_c),
    ):
        low = level.astype(BF16).astype(F32)
        factor = jnp.exp(low - level) * weight
        grads = (factor * g32).astype(BF16)
        corr = (factor * align).astype(BF16).astype(F32)
        column_id = lax.broadcasted_iota(jnp.int32, (picked, 2 * D), 1)
        across = jnp.where(column_id == 0, corr, low).T
        redo = jnp.exp(masked - across[1:2])
        dscore = (redo * (dot_t(vext, grads) - across[0:1])).astype(BF16)
        dk = dk + dot(dscore, q_b)
        dv = dv + dot(redo.astype(BF16), grads)
        dq = dq + dot(kext_t, dscore)
    both = jnp.concatenate([dk, dv], axis=1)
    dkv[own_b, :] = dkv[own_b, :] + both[:picked]
    oq[own_b, :] = oq[own_b, :] + jnp.concatenate([jnp.zeros_like(dq), dq * SCALE], axis=0).T
    parts_ref[...] = jnp.zeros_like(parts_ref)
    at = picked
    for j in range(1, near + far + 1):
        slot = pl.ds((team ^ j) * TEAM, TEAM)
        for i in range(rows // 64 if j <= near else 1):
            piece = both[at : at + 8 * TEAM].reshape(TEAM, 8, 2 * D)
            parts_ref[slot, :, i * 2 * D : (i + 1) * 2 * D] = piece.astype(BF16)
            at += 8 * TEAM
    for t, ref in enumerate((o0, o1, o2, o3)):
        at = slice(2 * t * rows, 2 * (t + 1) * rows)
        ref[:, : 2 * D] = dkv[at, :].astype(BF16)
        ref[:, 2 * D :] = oq[at, :].astype(BF16)


def middle_body(m0, m2, m3, m1, parts_ref, keep_ref, send_ref):
    rows = keep_ref.shape[1]
    for t, main in enumerate((m0, m1, m2, m3)):
        keep_ref[t] = main[:rows]
        send_ref[t] = main[rows:]


def unpack_body(near, keep_ref, recv_ref, parts_ref, out_ref, dq_ref, dk_ref, dv_ref, heads_ref, wide):
    chip, column = place()
    for side in range(2):

        @pl.when(column == side)
        def _():
            for h in range(HEADS):
                source = keep_ref if h // 3 == side else recv_ref
                heads_ref[h] = source[(h % 3 + h // 3) ^ chip]

    rows = keep_ref.shape[1]
    team = my_team()
    teams = parts_ref.shape[0] // TEAM
    for h in range(HEADS):
        member = 2 * (h % 3 + h // 3) + h // 3
        wide[h] = heads_ref[h, :, : 2 * D].astype(F32)
        for j in range(1, teams):
            part = parts_ref[(team ^ j) * TEAM + member].astype(F32)
            pieces = [part[:, i * 2 * D : (i + 1) * 2 * D] for i in range(rows // 64)]
            if j <= near:
                chosen, part = pl.ds(h, rows // 8, stride=8), jnp.concatenate(pieces, axis=0)
            else:
                chosen, part = pl.ds(h, rows // 64, stride=64), pieces[0][: rows // 64]
            wide[h, chosen, :] = wide[h, chosen, :] + part
    for at, ref in ((0, dk_ref), (1, dv_ref)):
        ref[...] = jnp.concatenate(
            [wide[h, :, at * D : (at + 1) * D] for h in range(HEADS)], axis=1
        ).astype(BF16)
    for at, ref in ((2, out_ref), (3, dq_ref)):
        ref[...] = jnp.concatenate(
            [heads_ref[h, :, at * D : (at + 1) * D] for h in range(HEADS)], axis=1
        )


def exchange(slots):
    slots = lax.all_to_all(slots, AXES, 0, 0)
    return slots


def shards(query_rows, key_rows, value_rows, out_grad):
    rows = query_rows.shape[0]
    width = 4 * D
    count = lax.axis_size("outer") * lax.axis_size("inner")
    near = 2 * lax.axis_size("inner") // TEAM - 1
    far = count // TEAM - 1 - near
    to_owner = lambda source, target: owns(target)
    from_owner = lambda source, target: owns(source)
    total = TEAM * rows

    block = ((4, rows, width), BF16)
    slots_shape = ((count, 8, rows // 64 * 2 * D), BF16)
    given = pltpu.VMEM((rows, HEADS * D), BF16)
    keep, send, slots = call(
        functools.partial(pack_body, near),
        [block, block, slots_shape],
        *[pltpu.with_memory_space_constraint(x, pltpu.HBM) for x in (query_rows, key_rows, value_rows, out_grad)],
        scratch=[pltpu.VMEM((HEADS, rows, width), BF16)] + [given] * 4
        + [
            pltpu.VMEM((rows, 2 * D), F32),
            pltpu.VMEM((64, 2 * D), F32),
            pltpu.VMEM((2, HEADS, 8, rows // 64 * 2 * D), BF16),
            pltpu.SemaphoreType.DMA((4,)),
        ],
        specs=[HBM] * 4,
    )
    recv = move(send, 1)
    s1, s2, s3 = call(regroup_body, [((2 * rows, width), BF16)] * 3, keep, recv)
    got = [move(s, 2 * t, to_owner) for t, s in ((1, s1), (2, s2), (3, s3))]
    slots = exchange(slots)
    *mains, parts = call(
        functools.partial(main_body, near, far),
        [((2 * rows, width), BF16)] * 4 + [slots_shape],
        keep,
        recv,
        got[1],
        got[2],
        got[0],
        slots,
        scratch=[
            pltpu.VMEM((total, 2 * D), F32),
            pltpu.VMEM((total, 2 * D), F32),
            pltpu.VMEM((total, D), BF16),
            pltpu.VMEM((total, D), BF16),
            pltpu.VMEM((D, total), BF16),
            pltpu.VMEM((D, total), F32),
            pltpu.VMEM((2 * D, total), BF16),
            pltpu.VMEM((total, total), F32),
            pltpu.VMEM((total, 2 * D), F32),
            pltpu.VMEM((total, 2 * D), F32),
            pltpu.VMEM((total, 2 * D), F32),
            pltpu.VMEM((2 * D, total), F32),
            pltpu.VMEM((total, 2 * D), F32),
        ],
    )
    back = [mains[0]] + [move(mains[t], 2 * t, from_owner) for t in (1, 2, 3)]
    parts = exchange(parts)
    keep, send = call(
        middle_body, [block, block], back[0], back[2], back[3], back[1], parts, specs=[VMEM] * 4 + [HBM]
    )
    recv = move(send, 1)
    out = ((rows, HEADS * D), BF16)
    return tuple(
        call(
            functools.partial(unpack_body, near), [out] * 4, keep, recv, parts,
            scratch=[
                pltpu.VMEM((HEADS, rows, width), BF16),
                pltpu.VMEM((HEADS, rows, 2 * D), F32),
            ],
        )
    )


def solution(mesh):
    spec = P(AXES, None)
    return jax.shard_map(
        shards, mesh=mesh, in_specs=(spec,) * 4, out_specs=(spec,) * 4, check_vma=False
    )
```

```python
import functools

import jax
import jax.numpy as jnp
from jax import lax
from jax.experimental import pallas as pl
from jax.experimental.pallas import tpu as pltpu
from jax.sharding import PartitionSpec as P

HEADS = 6
D = 64
SCALE = float(D) ** (-0.5)
AXES = ("outer", "inner")
TEAM = 8
NONE = -1e30
HINT = 10**11
F32 = jnp.float32
BF16 = jnp.bfloat16
VMEM = pl.BlockSpec(memory_space=pltpu.VMEM)
HBM = pl.BlockSpec(memory_space=pltpu.HBM)


def dot(a, b):
    return jnp.dot(a, b, preferred_element_type=F32)


def dot_t(a, b):
    return lax.dot_general(a, b, (((1,), (1,)), ((), ())), preferred_element_type=F32)


def place():
    member = lax.rem(lax.axis_index("inner"), TEAM)
    return lax.div(member, 2), lax.rem(member, 2)


def head_at(chip, column):
    return 3 * column + jnp.clip(chip - column, 0, 2)


def owns(member):
    return 0 <= member // 2 - member % 2 <= 2


def move(value, mask, keep=lambda source, target: True):
    count = lax.axis_size("outer") * lax.axis_size("inner")
    pairs = [(s, s ^ mask) for s in range(count) if keep(s % TEAM, (s ^ mask) % TEAM)]
    return lax.ppermute(value, AXES, pairs)


def call(body, outs, *args, scratch=(), specs=None, cost=None):
    return pl.pallas_call(
        body,
        out_shape=[jax.ShapeDtypeStruct(shape, dtype) for shape, dtype in outs],
        in_specs=specs or [VMEM] * len(args),
        out_specs=[VMEM] * len(outs),
        scratch_shapes=list(scratch),
        cost_estimate=cost
        and pl.CostEstimate(flops=cost, transcendentals=0, bytes_accessed=2**20),
        compiler_params=pltpu.CompilerParams(vmem_limit_bytes=48 * 2**20),
    )(*args)


def side_by_side(x):
    return jnp.concatenate([x[at : at + 8] for at in range(0, x.shape[0], 8)], axis=1)


def pack_body(
    near,
    q_hbm,
    k_hbm,
    v_hbm,
    g_hbm,
    keep_ref,
    send_ref,
    slots_ref,
    heads_ref,
    q_ref,
    k_ref,
    v_ref,
    g_ref,
    wide,
    thin,
    picks,
    sems,
):
    copies = [
        pltpu.make_async_copy(source, target, sems.at[i])
        for i, (source, target) in enumerate(
            ((k_hbm, k_ref), (v_hbm, v_ref), (q_hbm, q_ref), (g_hbm, g_ref))
        )
    ]
    for copy in copies:
        copy.start()
    for copy in copies:
        copy.wait()
    chip, column = place()
    q = (q_ref[...].astype(F32) * SCALE).astype(BF16)
    k, v, g = k_ref[...], v_ref[...], g_ref[...]
    picked = k.shape[0] // 8
    thin[...] = jnp.zeros_like(thin)
    for h in range(HEADS):
        cols = slice(h * D, (h + 1) * D)
        pair = jnp.concatenate([k[:, cols], v[:, cols]], axis=1)
        heads_ref[h, :, : 2 * D] = pair
        heads_ref[h, :, 2 * D :] = jnp.concatenate([q[:, cols], g[:, cols]], axis=1)
        wide[...] = pair.astype(F32)
        chosen = wide[pl.ds(h, picked, stride=8), :]
        picks[0, h] = side_by_side(chosen).astype(BF16)
        thin[:picked] = chosen
        few = thin[pl.ds(0, 8, stride=8), :]
        picks[1, h] = side_by_side(
            jnp.concatenate([few, jnp.zeros((picked - 8, 2 * D), F32)], axis=0)
        ).astype(BF16)
    for t in range(4):
        keep_ref[t] = heads_ref[head_at(chip ^ t, column)]
        send_ref[t] = heads_ref[head_at(chip ^ t, 1 - column)]
    segment = lax.div(my_team(), near + 1)
    for team in range(slots_ref.shape[0] // TEAM):
        other = (segment != team // (near + 1)).astype(jnp.int32)
        for member in range(TEAM):
            head = 3 * (member % 2) + min(max(member // 2 - member % 2, 0), 2)
            slots_ref[team * TEAM + member] = picks[other, head]


def my_team():
    teams_in = lax.axis_size("inner") // TEAM
    return lax.axis_index("outer") * teams_in + lax.div(lax.axis_index("inner"), TEAM)


def regroup_body(keep_ref, recv_ref, s1, s2, s3):
    rows = keep_ref.shape[1]
    for t, ref in enumerate((s1, s2, s3), 1):
        ref[:rows] = keep_ref[t]
        ref[rows:] = recv_ref[t]


def main_body(
    near,
    far,
    keep_ref,
    recv_ref,
    r2,
    r3,
    r1,
    slots_ref,
    o0,
    o1,
    o2,
    o3,
    parts_ref,
    *scratch,
):
    (xa, xb, keys, vals, qt, gt, kvt, st, oq, dkv, z, zt, stats) = scratch
    chip, column = place()
    head = head_at(chip, column)
    rows = keep_ref.shape[1]
    total = TEAM * rows
    picked = total // 8
    own_b = pl.ds(head, picked, stride=8)

    blocks = [keep_ref[0], recv_ref[0]]
    for ref in (r1, r2, r3):
        blocks += [ref[:rows], ref[rows:]]
    for i, block in enumerate(blocks):
        at = slice(i * rows, (i + 1) * rows)
        keys[at] = block[:, :D]
        vals[at] = block[:, D : 2 * D]
        xa[at] = block[:, : 2 * D].astype(F32)
        xb[at] = block[:, 2 * D :].astype(F32)
    kvt[...] = xa[...].T.astype(BF16)
    flipped = xb[...].T
    qt[...] = flipped[:D].astype(BF16)
    gt[...] = flipped[D:]

    mine = xb[own_b, :].astype(BF16)
    team = my_team()
    pieces = [xa[own_b, :]]
    for j in range(1, near + far + 1):
        slot = pl.ds((team ^ j) * TEAM, TEAM)
        for i in range(rows // 64 if j <= near else 1):
            part = slots_ref[slot, :, i * 2 * D : (i + 1) * 2 * D]
            pieces.append(part.astype(F32).reshape(-1, 2 * D))
    other = jnp.concatenate(pieces, axis=0).astype(BF16)
    kext, vext = other[:, :D], other[:, D:]
    q_b, g_b = mine[:, :D], mine[:, D:]
    extent = other.shape[0]
    row = lax.broadcasted_iota(jnp.int32, (extent, 1), 0)
    use_b = row < (near + 1) * picked
    use_c = lax.rem(row, 8) < jnp.where(use_b, 1, rows // 64)
    scores = dot_t(kext, q_b)

    def branch(use):
        masked = jnp.where(use, scores, NONE)
        highest = jnp.max(masked, axis=0, keepdims=True)
        level = highest + jnp.log(jnp.sum(jnp.exp(masked - highest), axis=0, keepdims=True))
        probs = jnp.exp(masked - level).astype(BF16)
        return level, masked, probs

    level_b, masked_b, probs_b = branch(use_b)
    level_c, masked_c, probs_c = branch(use_c)
    vext_t = vext.astype(F32).T.astype(BF16)
    kext_t = kext.astype(F32).T.astype(BF16)
    part_b = dot(vext_t, probs_b)
    part_c = dot(vext_t, probs_c)
    lane = lax.broadcasted_iota(jnp.int32, (1, picked), 1)
    in_c = lax.rem(lane, 8) == 0
    level_in = jnp.where(in_c, level_c, NONE)
    top = jnp.maximum(level_b, level_in)
    level_bc = top + jnp.log(jnp.exp(level_b - top) + jnp.exp(level_in - top))
    part_bc = jnp.exp(level_b - level_bc) * part_b + jnp.exp(level_in - level_bc) * part_c
    lanes = lax.broadcasted_iota(jnp.int32, z.shape, 1)
    z[...] = jnp.where(lanes < D, 0.0, NONE)
    z[own_b, :] = jnp.concatenate([part_bc, jnp.broadcast_to(level_bc, (D, picked))], axis=0).T
    zt[...] = z[...].T

    tile = total
    chunk = 2 * rows
    dkv[...] = jnp.zeros_like(dkv)
    zero = jnp.zeros((D, tile), BF16)

    def fold(x, op):
        return op(x.reshape(-1, 8, x.shape[1]), axis=0)

    def one_tile(t, carry):
        here = pl.ds(pl.multiple_of(t * tile, tile), tile)
        q_t = qt[:, here]
        top = jnp.full((8, tile), NONE, F32)
        for at in range(0, total, chunk):
            s = dot(keys[at : at + chunk, :], q_t)
            st[at : at + chunk, :] = s
            top = jnp.maximum(top, fold(s, jnp.max))
        top = jnp.max(top, axis=0, keepdims=True)
        mass = jnp.zeros((8, tile), F32)
        for at in range(0, total, chunk):
            e = jnp.exp(st[at : at + chunk, :] - top)
            st[at : at + chunk, :] = e
            mass = mass + fold(e, jnp.sum)
        mass = jnp.sum(mass, axis=0, keepdims=True)
        level = top + jnp.log(mass)
        norm = 1.0 / mass
        part = [jnp.zeros((D, tile), F32)] * 2
        for i, at in enumerate(range(0, total, chunk)):
            probs = (st[at : at + chunk, :] * norm).astype(BF16)
            part[i % 2] = part[i % 2] + dot(kvt[D:, at : at + chunk], probs)
        level_o = zt[D : D + 1, here]
        highest = jnp.maximum(level, level_o)
        overall = highest + jnp.log(jnp.exp(level - highest) + jnp.exp(level_o - highest))
        weight = jnp.exp(level - overall)
        combined = weight * (part[0] + part[1]) + jnp.exp(level_o - overall) * zt[:D, here]
        g_t = gt[:, here]
        align = jnp.sum(g_t * combined, axis=0, keepdims=True)
        low = level.astype(BF16).astype(F32)
        factor = jnp.exp(low - level) * weight
        grads = (factor * g_t).astype(BF16)
        corr = (factor * align).astype(BF16).astype(F32)
        lift = jnp.exp(top - low)
        right = jnp.concatenate(
            [jnp.concatenate([q_t, zero], axis=1), jnp.concatenate([zero, grads], axis=1)], axis=0
        )
        dq = [jnp.zeros((D, tile), F32)] * 2
        for i, at in enumerate(range(0, total, chunk)):
            redo = st[at : at + chunk, :] * lift
            dprob = dot(vals[at : at + chunk, :], grads)
            dscore = (redo * (dprob - corr)).astype(BF16)
            dq[i % 2] = dq[i % 2] + dot(kvt[:D, at : at + chunk], dscore)
            dkv[at : at + chunk, :] += dot_t(
                jnp.concatenate([dscore, redo.astype(BF16)], axis=1), right
            )
        oq[here, :] = jnp.concatenate([combined, (dq[0] + dq[1]) * SCALE], axis=0).T
        stats[here, :] = jnp.concatenate(
            [align, overall, jnp.zeros((126, tile), F32)], axis=0
        ).T
        return carry

    lax.fori_loop(0, total // tile, one_tile, 0)

    numbers = stats[own_b, :]
    align, overall = numbers[:, 0:1], numbers[:, 1:2]
    g32 = g_b.astype(F32)
    levels_t = jnp.concatenate(
        [level_b, level_c, level_in, jnp.zeros((125, picked), F32)], axis=0
    ).T
    dk = jnp.zeros((extent, D), F32)
    dv = jnp.zeros((extent, D), F32)
    dq = jnp.zeros((D, picked), F32)
    for level, weight, masked in (
        (levels_t[:, 0:1], jnp.exp(levels_t[:, 0:1] - overall), masked_b),
        (levels_t[:, 1:2], jnp.exp(levels_t[:, 2:3] - overall), masked_c),
    ):
        low = level.astype(BF16).astype(F32)
        factor = jnp.exp(low - level) * weight
        grads = (factor * g32).astype(BF16)
        corr = (factor * align).astype(BF16).astype(F32)
        column_id = lax.broadcasted_iota(jnp.int32, (picked, 2 * D), 1)
        across = jnp.where(column_id == 0, corr, low).T
        redo = jnp.exp(masked - across[1:2])
        dscore = (redo * (dot_t(vext, grads) - across[0:1])).astype(BF16)
        dk = dk + dot(dscore, q_b)
        dv = dv + dot(redo.astype(BF16), grads)
        dq = dq + dot(kext_t, dscore)
    both = jnp.concatenate([dk, dv], axis=1)
    dkv[own_b, :] = dkv[own_b, :] + both[:picked]
    oq[own_b, :] = oq[own_b, :] + jnp.concatenate([jnp.zeros_like(dq), dq * SCALE], axis=0).T
    parts_ref[...] = jnp.zeros_like(parts_ref)
    at = picked
    for j in range(1, near + far + 1):
        slot = pl.ds((team ^ j) * TEAM, TEAM)
        for i in range(rows // 64 if j <= near else 1):
            piece = both[at : at + 8 * TEAM].reshape(TEAM, 8, 2 * D)
            parts_ref[slot, :, i * 2 * D : (i + 1) * 2 * D] = piece.astype(BF16)
            at += 8 * TEAM
    for t, ref in enumerate((o0, o1, o2, o3)):
        at = slice(2 * t * rows, 2 * (t + 1) * rows)
        ref[:, : 2 * D] = dkv[at, :].astype(BF16)
        ref[:, 2 * D :] = oq[at, :].astype(BF16)


def middle_body(m0, m2, m3, m1, keep_ref, send_ref):
    rows = keep_ref.shape[1]
    for t, main in enumerate((m0, m1, m2, m3)):
        keep_ref[t] = main[:rows]
        send_ref[t] = main[rows:]


def order_body(keep_ref, out_ref):
    chip, column = place()
    for i in range(3):
        out_ref[i] = keep_ref[(i + column) ^ chip]


def unpack_body(near, keep_ref, recv_ref, parts_ref, out_ref, dq_ref, dk_ref, dv_ref, heads_ref, wide):
    chip, column = place()
    for side in range(2):

        @pl.when(column == side)
        def _():
            for h in range(HEADS):
                if h // 3 == side:
                    heads_ref[h] = keep_ref[h % 3]
                else:
                    heads_ref[h] = recv_ref[(h % 3 + h // 3) ^ chip]

    rows = keep_ref.shape[1]
    team = my_team()
    teams = parts_ref.shape[0] // TEAM
    for h in range(HEADS):
        member = 2 * (h % 3 + h // 3) + h // 3
        wide[h] = heads_ref[h, :, : 2 * D].astype(F32)
        for j in range(1, teams):
            part = parts_ref[(team ^ j) * TEAM + member].astype(F32)
            pieces = [part[:, i * 2 * D : (i + 1) * 2 * D] for i in range(rows // 64)]
            if j <= near:
                chosen, part = pl.ds(h, rows // 8, stride=8), jnp.concatenate(pieces, axis=0)
            else:
                chosen, part = pl.ds(h, rows // 64, stride=64), pieces[0][: rows // 64]
            wide[h, chosen, :] = wide[h, chosen, :] + part
    for at, ref in ((0, dk_ref), (1, dv_ref)):
        ref[...] = jnp.concatenate(
            [wide[h, :, at * D : (at + 1) * D] for h in range(HEADS)], axis=1
        ).astype(BF16)
    for at, ref in ((2, out_ref), (3, dq_ref)):
        ref[...] = jnp.concatenate(
            [heads_ref[h, :, at * D : (at + 1) * D] for h in range(HEADS)], axis=1
        )


def shards(query_rows, key_rows, value_rows, out_grad):
    rows = query_rows.shape[0]
    width = 4 * D
    count = lax.axis_size("outer") * lax.axis_size("inner")
    near = 2 * lax.axis_size("inner") // TEAM - 1
    far = count // TEAM - 1 - near
    to_owner = lambda source, target: owns(target)
    from_owner = lambda source, target: owns(source)
    total = TEAM * rows

    block = ((4, rows, width), BF16)
    slots_shape = ((count, 8, rows // 64 * 2 * D), BF16)
    given = pltpu.VMEM((rows, HEADS * D), BF16)
    keep, send, slots = call(
        functools.partial(pack_body, near),
        [block, block, slots_shape],
        *[pltpu.with_memory_space_constraint(x, pltpu.HBM) for x in (query_rows, key_rows, value_rows, out_grad)],
        scratch=[pltpu.VMEM((HEADS, rows, width), BF16)] + [given] * 4
        + [
            pltpu.VMEM((rows, 2 * D), F32),
            pltpu.VMEM((64, 2 * D), F32),
            pltpu.VMEM((2, HEADS, 8, rows // 64 * 2 * D), BF16),
            pltpu.SemaphoreType.DMA((4,)),
        ],
        specs=[HBM] * 4,
    )
    recv = move(send, 1)
    s1, s2, s3 = call(regroup_body, [((2 * rows, width), BF16)] * 3, keep, recv)
    got = [move(s, 2 * t, to_owner) for t, s in ((1, s1), (2, s2), (3, s3))]
    slots = lax.all_to_all(slots, AXES, 0, 0)
    *mains, parts = call(
        functools.partial(main_body, near, far),
        [((2 * rows, width), BF16)] * 4 + [slots_shape],
        keep,
        recv,
        got[1],
        got[2],
        got[0],
        slots,
        scratch=[
            pltpu.VMEM((total, 2 * D), F32),
            pltpu.VMEM((total, 2 * D), F32),
            pltpu.VMEM((total, D), BF16),
            pltpu.VMEM((total, D), BF16),
            pltpu.VMEM((D, total), BF16),
            pltpu.VMEM((D, total), F32),
            pltpu.VMEM((2 * D, total), BF16),
            pltpu.VMEM((total, total), F32),
            pltpu.VMEM((total, 2 * D), F32),
            pltpu.VMEM((total, 2 * D), F32),
            pltpu.VMEM((total, 2 * D), F32),
            pltpu.VMEM((2 * D, total), F32),
            pltpu.VMEM((total, 2 * D), F32),
        ],
    )
    back = [mains[0]] + [move(mains[t], 2 * t, from_owner) for t in (1, 2, 3)]
    parts = lax.all_to_all(parts, AXES, 0, 0)
    keep, send = call(
        middle_body, [block, block], back[0], back[2], back[3], back[1], cost=HINT
    )
    recv = move(send, 1)
    (mine,) = call(order_body, [((3, rows, width), BF16)], keep, cost=HINT)
    out = ((rows, HEADS * D), BF16)
    return tuple(
        call(
            functools.partial(unpack_body, near), [out] * 4, mine, recv, parts,
            scratch=[
                pltpu.VMEM((HEADS, rows, width), BF16),
                pltpu.VMEM((HEADS, rows, 2 * D), F32),
            ],
        )
    )


def solution(mesh):
    spec = P(AXES, None)
    return jax.shard_map(
        shards, mesh=mesh, in_specs=(spec,) * 4, out_specs=(spec,) * 4, check_vma=False
    )
```

```python
import functools

import jax
import jax.numpy as jnp
from jax import lax
from jax.experimental import pallas as pl
from jax.experimental.pallas import tpu as pltpu
from jax.sharding import PartitionSpec as P

HEADS = 6
D = 64
SCALE = float(D) ** (-0.5)
AXES = ("outer", "inner")
TEAM = 8
NONE = -1e30
HINT = 8 * 10**9
F32 = jnp.float32
BF16 = jnp.bfloat16
VMEM = pl.BlockSpec(memory_space=pltpu.VMEM)
HBM = pl.BlockSpec(memory_space=pltpu.HBM)


def dot(a, b):
    return jnp.dot(a, b, preferred_element_type=F32)


def dot_t(a, b):
    return lax.dot_general(a, b, (((1,), (1,)), ((), ())), preferred_element_type=F32)


def place():
    member = lax.rem(lax.axis_index("inner"), TEAM)
    return lax.div(member, 2), lax.rem(member, 2)


def head_at(chip, column):
    return 3 * column + jnp.clip(chip - column, 0, 2)


def owns(member):
    return 0 <= member // 2 - member % 2 <= 2


def move(value, mask, keep=lambda source, target: True):
    count = lax.axis_size("outer") * lax.axis_size("inner")
    pairs = [(s, s ^ mask) for s in range(count) if keep(s % TEAM, (s ^ mask) % TEAM)]
    return lax.ppermute(value, AXES, pairs)


def call(body, outs, *args, scratch=(), specs=None, cost=None, outs_in=None):
    return pl.pallas_call(
        body,
        out_shape=[jax.ShapeDtypeStruct(shape, dtype) for shape, dtype in outs],
        in_specs=specs or [VMEM] * len(args),
        out_specs=outs_in or [VMEM] * len(outs),
        scratch_shapes=list(scratch),
        cost_estimate=cost
        and pl.CostEstimate(flops=cost, transcendentals=0, bytes_accessed=2**20),
        compiler_params=pltpu.CompilerParams(vmem_limit_bytes=48 * 2**20),
    )(*args)


def side_by_side(x):
    return jnp.concatenate([x[at : at + 8] for at in range(0, x.shape[0], 8)], axis=1)


def pack_body(
    near,
    q_hbm,
    k_hbm,
    v_hbm,
    g_hbm,
    keep_ref,
    send_ref,
    slots_hbm,
    heads_ref,
    q_ref,
    k_ref,
    v_ref,
    g_ref,
    wide,
    thin,
    picks,
    slots_ref,
    sems,
):
    copies = [
        pltpu.make_async_copy(source, target, sems.at[i])
        for i, (source, target) in enumerate(
            ((k_hbm, k_ref), (v_hbm, v_ref), (q_hbm, q_ref), (g_hbm, g_ref))
        )
    ]
    for copy in copies:
        copy.start()
    chip, column = place()
    copies[0].wait()
    copies[1].wait()
    k, v = k_ref[...], v_ref[...]
    picked = k.shape[0] // 8
    thin[...] = jnp.zeros_like(thin)
    for h in range(HEADS):
        cols = slice(h * D, (h + 1) * D)
        pair = jnp.concatenate([k[:, cols], v[:, cols]], axis=1)
        heads_ref[h, :, : 2 * D] = pair
        wide[...] = pair.astype(F32)
        chosen = wide[pl.ds(h, picked, stride=8), :]
        picks[0, h] = side_by_side(chosen).astype(BF16)
        thin[:picked] = chosen
        few = thin[pl.ds(0, 8, stride=8), :]
        picks[1, h] = side_by_side(
            jnp.concatenate([few, jnp.zeros((picked - 8, 2 * D), F32)], axis=0)
        ).astype(BF16)
    segment = lax.div(my_team(), near + 1)
    for team in range(slots_ref.shape[0] // TEAM):
        other = (segment != team // (near + 1)).astype(jnp.int32)
        for member in range(TEAM):
            head = 3 * (member % 2) + min(max(member // 2 - member % 2, 0), 2)
            slots_ref[team * TEAM + member] = picks[other, head]
    out = pltpu.make_async_copy(slots_ref, slots_hbm, sems.at[4])
    out.start()
    copies[2].wait()
    copies[3].wait()
    q = (q_ref[...].astype(F32) * SCALE).astype(BF16)
    g = g_ref[...]
    for h in range(HEADS):
        cols = slice(h * D, (h + 1) * D)
        heads_ref[h, :, 2 * D :] = jnp.concatenate([q[:, cols], g[:, cols]], axis=1)
    for t in range(4):
        keep_ref[t] = heads_ref[head_at(chip ^ t, column)]
        send_ref[t] = heads_ref[head_at(chip ^ t, 1 - column)]
    out.wait()


def my_team():
    teams_in = lax.axis_size("inner") // TEAM
    return lax.axis_index("outer") * teams_in + lax.div(lax.axis_index("inner"), TEAM)


def regroup_body(keep_ref, recv_ref, s1, s2, s3):
    rows = keep_ref.shape[1]
    for t, ref in enumerate((s1, s2, s3), 1):
        ref[:rows] = keep_ref[t]
        ref[rows:] = recv_ref[t]


def main_body(
    near,
    far,
    keep_ref,
    recv_ref,
    r2,
    r3,
    r1,
    slots_ref,
    o0,
    o1,
    o2,
    o3,
    parts_hbm,
    *scratch,
):
    (xa, xb, keys, vals, qt, gt, kvt, st, oq, dkv, z, zt, stats, parts_ref, sems) = scratch
    chip, column = place()
    head = head_at(chip, column)
    rows = keep_ref.shape[1]
    total = TEAM * rows
    picked = total // 8
    own_b = pl.ds(head, picked, stride=8)

    blocks = [keep_ref[0], recv_ref[0]]
    for ref in (r1, r2, r3):
        blocks += [ref[:rows], ref[rows:]]
    for i, block in enumerate(blocks):
        at = slice(i * rows, (i + 1) * rows)
        keys[at] = block[:, :D]
        vals[at] = block[:, D : 2 * D]
        xa[at] = block[:, : 2 * D].astype(F32)
        xb[at] = block[:, 2 * D :].astype(F32)
    kvt[...] = xa[...].T.astype(BF16)
    flipped = xb[...].T
    qt[...] = flipped[:D].astype(BF16)
    gt[...] = flipped[D:]

    mine = xb[own_b, :].astype(BF16)
    team = my_team()
    pieces = [xa[own_b, :]]
    for j in range(1, near + far + 1):
        slot = pl.ds((team ^ j) * TEAM, TEAM)
        for i in range(rows // 64 if j <= near else 1):
            part = slots_ref[slot, :, i * 2 * D : (i + 1) * 2 * D]
            pieces.append(part.astype(F32).reshape(-1, 2 * D))
    other = jnp.concatenate(pieces, axis=0).astype(BF16)
    kext, vext = other[:, :D], other[:, D:]
    q_b, g_b = mine[:, :D], mine[:, D:]
    extent = other.shape[0]
    row = lax.broadcasted_iota(jnp.int32, (extent, 1), 0)
    use_b = row < (near + 1) * picked
    use_c = lax.rem(row, 8) < jnp.where(use_b, 1, rows // 64)
    scores = dot_t(kext, q_b)

    def branch(use):
        masked = jnp.where(use, scores, NONE)
        highest = jnp.max(masked, axis=0, keepdims=True)
        level = highest + jnp.log(jnp.sum(jnp.exp(masked - highest), axis=0, keepdims=True))
        probs = jnp.exp(masked - level).astype(BF16)
        return level, masked, probs

    level_b, masked_b, probs_b = branch(use_b)
    level_c, masked_c, probs_c = branch(use_c)
    vext_t = vext.astype(F32).T.astype(BF16)
    kext_t = kext.astype(F32).T.astype(BF16)
    part_b = dot(vext_t, probs_b)
    part_c = dot(vext_t, probs_c)
    lane = lax.broadcasted_iota(jnp.int32, (1, picked), 1)
    in_c = lax.rem(lane, 8) == 0
    level_in = jnp.where(in_c, level_c, NONE)
    top = jnp.maximum(level_b, level_in)
    level_bc = top + jnp.log(jnp.exp(level_b - top) + jnp.exp(level_in - top))
    part_bc = jnp.exp(level_b - level_bc) * part_b + jnp.exp(level_in - level_bc) * part_c
    lanes = lax.broadcasted_iota(jnp.int32, z.shape, 1)
    z[...] = jnp.where(lanes < D, 0.0, NONE)
    z[own_b, :] = jnp.concatenate([part_bc, jnp.broadcast_to(level_bc, (D, picked))], axis=0).T
    zt[...] = z[...].T

    tile = total
    chunk = 2 * rows
    dkv[...] = jnp.zeros_like(dkv)
    zero = jnp.zeros((D, tile), BF16)

    def fold(x, op):
        return op(x.reshape(-1, 8, x.shape[1]), axis=0)

    def one_tile(t, carry):
        here = pl.ds(pl.multiple_of(t * tile, tile), tile)
        q_t = qt[:, here]
        top = jnp.full((8, tile), NONE, F32)
        for at in range(0, total, chunk):
            s = dot(keys[at : at + chunk, :], q_t)
            st[at : at + chunk, :] = s
            top = jnp.maximum(top, fold(s, jnp.max))
        top = jnp.max(top, axis=0, keepdims=True)
        mass = jnp.zeros((8, tile), F32)
        for at in range(0, total, chunk):
            e = jnp.exp(st[at : at + chunk, :] - top)
            st[at : at + chunk, :] = e
            mass = mass + fold(e, jnp.sum)
        mass = jnp.sum(mass, axis=0, keepdims=True)
        level = top + jnp.log(mass)
        norm = 1.0 / mass
        part = [jnp.zeros((D, tile), F32)] * 2
        for i, at in enumerate(range(0, total, chunk)):
            probs = (st[at : at + chunk, :] * norm).astype(BF16)
            part[i % 2] = part[i % 2] + dot(kvt[D:, at : at + chunk], probs)
        level_o = zt[D : D + 1, here]
        highest = jnp.maximum(level, level_o)
        overall = highest + jnp.log(jnp.exp(level - highest) + jnp.exp(level_o - highest))
        weight = jnp.exp(level - overall)
        combined = weight * (part[0] + part[1]) + jnp.exp(level_o - overall) * zt[:D, here]
        g_t = gt[:, here]
        align = jnp.sum(g_t * combined, axis=0, keepdims=True)
        low = level.astype(BF16).astype(F32)
        factor = jnp.exp(low - level) * weight
        grads = (factor * g_t).astype(BF16)
        corr = (factor * align).astype(BF16).astype(F32)
        lift = jnp.exp(top - low)
        right = jnp.concatenate(
            [jnp.concatenate([q_t, zero], axis=1), jnp.concatenate([zero, grads], axis=1)], axis=0
        )
        dq = [jnp.zeros((D, tile), F32)] * 2
        for i, at in enumerate(range(0, total, chunk)):
            redo = st[at : at + chunk, :] * lift
            dprob = dot(vals[at : at + chunk, :], grads)
            dscore = (redo * (dprob - corr)).astype(BF16)
            dq[i % 2] = dq[i % 2] + dot(kvt[:D, at : at + chunk], dscore)
            dkv[at : at + chunk, :] += dot_t(
                jnp.concatenate([dscore, redo.astype(BF16)], axis=1), right
            )
        oq[here, :] = jnp.concatenate([combined, (dq[0] + dq[1]) * SCALE], axis=0).T
        stats[here, :] = jnp.concatenate(
            [align, overall, jnp.zeros((126, tile), F32)], axis=0
        ).T
        return carry

    lax.fori_loop(0, total // tile, one_tile, 0)

    numbers = stats[own_b, :]
    align, overall = numbers[:, 0:1], numbers[:, 1:2]
    g32 = g_b.astype(F32)
    levels_t = jnp.concatenate(
        [level_b, level_c, level_in, jnp.zeros((125, picked), F32)], axis=0
    ).T
    dk = jnp.zeros((extent, D), F32)
    dv = jnp.zeros((extent, D), F32)
    dq = jnp.zeros((D, picked), F32)
    for level, weight, masked in (
        (levels_t[:, 0:1], jnp.exp(levels_t[:, 0:1] - overall), masked_b),
        (levels_t[:, 1:2], jnp.exp(levels_t[:, 2:3] - overall), masked_c),
    ):
        low = level.astype(BF16).astype(F32)
        factor = jnp.exp(low - level) * weight
        grads = (factor * g32).astype(BF16)
        corr = (factor * align).astype(BF16).astype(F32)
        column_id = lax.broadcasted_iota(jnp.int32, (picked, 2 * D), 1)
        across = jnp.where(column_id == 0, corr, low).T
        redo = jnp.exp(masked - across[1:2])
        dscore = (redo * (dot_t(vext, grads) - across[0:1])).astype(BF16)
        dk = dk + dot(dscore, q_b)
        dv = dv + dot(redo.astype(BF16), grads)
        dq = dq + dot(kext_t, dscore)
    both = jnp.concatenate([dk, dv], axis=1)
    dkv[own_b, :] = dkv[own_b, :] + both[:picked]
    oq[own_b, :] = oq[own_b, :] + jnp.concatenate([jnp.zeros_like(dq), dq * SCALE], axis=0).T
    parts_ref[...] = jnp.zeros_like(parts_ref)
    at = picked
    for j in range(1, near + far + 1):
        slot = pl.ds((team ^ j) * TEAM, TEAM)
        for i in range(rows // 64 if j <= near else 1):
            piece = both[at : at + 8 * TEAM].reshape(TEAM, 8, 2 * D)
            parts_ref[slot, :, i * 2 * D : (i + 1) * 2 * D] = piece.astype(BF16)
            at += 8 * TEAM
    out = pltpu.make_async_copy(parts_ref, parts_hbm, sems.at[0])
    out.start()
    for t, ref in enumerate((o0, o1, o2, o3)):
        at = slice(2 * t * rows, 2 * (t + 1) * rows)
        ref[:, : 2 * D] = dkv[at, :].astype(BF16)
        ref[:, 2 * D :] = oq[at, :].astype(BF16)
    out.wait()


def middle_body(m0, m2, m3, m1, keep_ref, send_ref):
    rows = keep_ref.shape[1]
    for t, main in enumerate((m0, m1, m2, m3)):
        keep_ref[t] = main[:rows]
        send_ref[t] = main[rows:]


def order_body(keep_ref, out_ref):
    chip, column = place()
    for i in range(3):
        out_ref[i] = keep_ref[(i + column) ^ chip]


def unpack_body(
    near,
    keep_ref,
    recv_ref,
    parts_ref,
    out_hbm,
    dq_hbm,
    dk_hbm,
    dv_hbm,
    heads_ref,
    wide,
    ready,
    sems,
):
    chip, column = place()
    for side in range(2):

        @pl.when(column == side)
        def _():
            for h in range(HEADS):
                if h // 3 == side:
                    heads_ref[h] = keep_ref[h % 3]
                else:
                    heads_ref[h] = recv_ref[(h % 3 + h // 3) ^ chip]

    leaving = []

    def leave(value, target):
        i = len(leaving)
        ready[i] = value
        leaving.append(pltpu.make_async_copy(ready.at[i], target, sems.at[i]))
        leaving[i].start()

    for at, target in ((2, out_hbm), (3, dq_hbm)):
        leave(
            jnp.concatenate([heads_ref[h, :, at * D : (at + 1) * D] for h in range(HEADS)], axis=1),
            target,
        )
    rows = keep_ref.shape[1]
    team = my_team()
    teams = parts_ref.shape[0] // TEAM
    for h in range(HEADS):
        wide[h] = heads_ref[h, :, : 2 * D].astype(F32)
    for h in range(HEADS):
        member = 2 * (h % 3 + h // 3) + h // 3
        for j in range(1, teams):
            part = parts_ref[(team ^ j) * TEAM + member].astype(F32)
            pieces = [part[:, i * 2 * D : (i + 1) * 2 * D] for i in range(rows // 64)]
            if j <= near:
                chosen, part = pl.ds(h, rows // 8, stride=8), jnp.concatenate(pieces, axis=0)
            else:
                chosen, part = pl.ds(h, rows // 64, stride=64), pieces[0][: rows // 64]
            wide[h, chosen, :] = wide[h, chosen, :] + part
    for at, target in ((0, dk_hbm), (1, dv_hbm)):
        leave(
            jnp.concatenate(
                [wide[h, :, at * D : (at + 1) * D] for h in range(HEADS)], axis=1
            ).astype(BF16),
            target,
        )
    for copy in leaving:
        copy.wait()


def shards(query_rows, key_rows, value_rows, out_grad):
    rows = query_rows.shape[0]
    width = 4 * D
    count = lax.axis_size("outer") * lax.axis_size("inner")
    near = 2 * lax.axis_size("inner") // TEAM - 1
    far = count // TEAM - 1 - near
    to_owner = lambda source, target: owns(target)
    from_owner = lambda source, target: owns(source)
    total = TEAM * rows

    block = ((4, rows, width), BF16)
    slots_shape = ((count, 8, rows // 64 * 2 * D), BF16)
    given = pltpu.VMEM((rows, HEADS * D), BF16)
    keep, send, slots = call(
        functools.partial(pack_body, near),
        [block, block, slots_shape],
        *[pltpu.with_memory_space_constraint(x, pltpu.HBM) for x in (query_rows, key_rows, value_rows, out_grad)],
        scratch=[pltpu.VMEM((HEADS, rows, width), BF16)] + [given] * 4
        + [
            pltpu.VMEM((rows, 2 * D), F32),
            pltpu.VMEM((64, 2 * D), F32),
            pltpu.VMEM((2, HEADS, 8, rows // 64 * 2 * D), BF16),
            pltpu.VMEM(*slots_shape),
            pltpu.SemaphoreType.DMA((5,)),
        ],
        specs=[HBM] * 4,
        outs_in=[VMEM, VMEM, HBM],
    )
    recv = move(send, 1)
    s1, s2, s3 = call(regroup_body, [((2 * rows, width), BF16)] * 3, keep, recv)
    got = [move(s, 2 * t, to_owner) for t, s in ((1, s1), (2, s2), (3, s3))]
    slots = lax.all_to_all(slots, AXES, 0, 0)
    *mains, parts = call(
        functools.partial(main_body, near, far),
        [((2 * rows, width), BF16)] * 4 + [slots_shape],
        keep,
        recv,
        got[1],
        got[2],
        got[0],
        slots,
        scratch=[
            pltpu.VMEM((total, 2 * D), F32),
            pltpu.VMEM((total, 2 * D), F32),
            pltpu.VMEM((total, D), BF16),
            pltpu.VMEM((total, D), BF16),
            pltpu.VMEM((D, total), BF16),
            pltpu.VMEM((D, total), F32),
            pltpu.VMEM((2 * D, total), BF16),
            pltpu.VMEM((total, total), F32),
            pltpu.VMEM((total, 2 * D), F32),
            pltpu.VMEM((total, 2 * D), F32),
            pltpu.VMEM((total, 2 * D), F32),
            pltpu.VMEM((2 * D, total), F32),
            pltpu.VMEM((total, 2 * D), F32),
            pltpu.VMEM(*slots_shape),
            pltpu.SemaphoreType.DMA((1,)),
        ],
        outs_in=[VMEM] * 4 + [HBM],
    )
    back = [mains[0]] + [move(mains[t], 2 * t, from_owner) for t in (1, 2, 3)]
    parts = lax.all_to_all(parts, AXES, 0, 0)
    keep, send = call(
        middle_body, [block, block], back[0], back[2], back[3], back[1], cost=HINT
    )
    recv = move(send, 1)
    (mine,) = call(order_body, [((3, rows, width), BF16)], keep, cost=HINT)
    out = ((rows, HEADS * D), BF16)
    return tuple(
        call(
            functools.partial(unpack_body, near), [out] * 4, mine, recv, parts,
            scratch=[
                pltpu.VMEM((HEADS, rows, width), BF16),
                pltpu.VMEM((HEADS, rows, 2 * D), F32),
                pltpu.VMEM((4, rows, HEADS * D), BF16),
                pltpu.SemaphoreType.DMA((4,)),
            ],
            outs_in=[HBM] * 4,
        )
    )


def solution(mesh):
    spec = P(AXES, None)
    return jax.shard_map(
        shards, mesh=mesh, in_specs=(spec,) * 4, out_specs=(spec,) * 4, check_vma=False
    )
```

```python
import functools

import jax
import jax.numpy as jnp
from jax import lax
from jax.experimental import pallas as pl
from jax.experimental.pallas import tpu as pltpu
from jax.sharding import PartitionSpec as P

HEADS = 6
D = 64
SCALE = float(D) ** (-0.5)
AXES = ("outer", "inner")
TEAM = 8
NONE = -1e30
HINT = 8 * 10**9
F32 = jnp.float32
BF16 = jnp.bfloat16
VMEM = pl.BlockSpec(memory_space=pltpu.VMEM)
HBM = pl.BlockSpec(memory_space=pltpu.HBM)


def dot(a, b):
    return jnp.dot(a, b, preferred_element_type=F32)


def dot_t(a, b):
    return lax.dot_general(a, b, (((1,), (1,)), ((), ())), preferred_element_type=F32)


def place():
    member = lax.rem(lax.axis_index("inner"), TEAM)
    return lax.div(member, 2), lax.rem(member, 2)


def head_at(chip, column):
    return 3 * column + jnp.clip(chip - column, 0, 2)


def owns(member):
    return 0 <= member // 2 - member % 2 <= 2


def move(value, mask, keep=lambda source, target: True):
    count = lax.axis_size("outer") * lax.axis_size("inner")
    pairs = [(s, s ^ mask) for s in range(count) if keep(s % TEAM, (s ^ mask) % TEAM)]
    return lax.ppermute(value, AXES, pairs)


def call(body, outs, *args, scratch=(), specs=None, cost=None, outs_in=None):
    return pl.pallas_call(
        body,
        out_shape=[jax.ShapeDtypeStruct(shape, dtype) for shape, dtype in outs],
        in_specs=specs or [VMEM] * len(args),
        out_specs=outs_in or [VMEM] * len(outs),
        scratch_shapes=list(scratch),
        cost_estimate=cost
        and pl.CostEstimate(flops=cost, transcendentals=0, bytes_accessed=2**20),
        compiler_params=pltpu.CompilerParams(vmem_limit_bytes=48 * 2**20),
    )(*args)


def side_by_side(x):
    return jnp.concatenate([x[at : at + 8] for at in range(0, x.shape[0], 8)], axis=1)


def pack_body(
    near,
    q_hbm,
    k_hbm,
    v_hbm,
    g_hbm,
    keep_ref,
    send_ref,
    slots_hbm,
    heads_ref,
    q_ref,
    k_ref,
    v_ref,
    g_ref,
    wide,
    thin,
    picks,
    slots_ref,
    sems,
):
    copies = [
        pltpu.make_async_copy(source, target, sems.at[i])
        for i, (source, target) in enumerate(
            ((k_hbm, k_ref), (v_hbm, v_ref), (q_hbm, q_ref), (g_hbm, g_ref))
        )
    ]
    for copy in copies:
        copy.start()
    chip, column = place()
    copies[0].wait()
    copies[1].wait()
    k, v = k_ref[...], v_ref[...]
    picked = k.shape[0] // 8
    thin[...] = jnp.zeros_like(thin)
    for h in range(HEADS):
        cols = slice(h * D, (h + 1) * D)
        pair = jnp.concatenate([k[:, cols], v[:, cols]], axis=1)
        heads_ref[h, :, : 2 * D] = pair
        wide[...] = pair.astype(F32)
        chosen = wide[pl.ds(h, picked, stride=8), :]
        picks[0, h] = side_by_side(chosen).astype(BF16)
        thin[:picked] = chosen
        few = thin[pl.ds(0, 8, stride=8), :]
        picks[1, h] = side_by_side(
            jnp.concatenate([few, jnp.zeros((picked - 8, 2 * D), F32)], axis=0)
        ).astype(BF16)
    segment = lax.div(my_team(), near + 1)
    for team in range(slots_ref.shape[0] // TEAM):
        other = (segment != team // (near + 1)).astype(jnp.int32)
        for member in range(TEAM):
            head = 3 * (member % 2) + min(max(member // 2 - member % 2, 0), 2)
            slots_ref[team * TEAM + member] = picks[other, head]
    out = pltpu.make_async_copy(slots_ref, slots_hbm, sems.at[4])
    out.start()
    copies[2].wait()
    copies[3].wait()
    q = (q_ref[...].astype(F32) * SCALE).astype(BF16)
    g = g_ref[...]
    for h in range(HEADS):
        cols = slice(h * D, (h + 1) * D)
        heads_ref[h, :, 2 * D :] = jnp.concatenate([q[:, cols], g[:, cols]], axis=1)
    for t in range(4):
        keep_ref[t] = heads_ref[head_at(chip ^ t, column)]
        send_ref[t] = heads_ref[head_at(chip ^ t, 1 - column)]
    out.wait()


def my_team():
    teams_in = lax.axis_size("inner") // TEAM
    return lax.axis_index("outer") * teams_in + lax.div(lax.axis_index("inner"), TEAM)


def regroup_body(keep_ref, recv_ref, s1, s2, s3):
    rows = keep_ref.shape[1]
    for t, ref in enumerate((s1, s2, s3), 1):
        ref[:rows] = keep_ref[t]
        ref[rows:] = recv_ref[t]


def main_body(
    near,
    far,
    keep_ref,
    recv_ref,
    r2,
    r1,
    r3,
    slots_ref,
    o0,
    o1,
    o2,
    o3,
    parts_hbm,
    *scratch,
):
    (xa, xb, keys, vals, qt, gt, kvt, st, oq, dkv, z, zt, stats, parts_ref, sems) = scratch
    chip, column = place()
    head = head_at(chip, column)
    rows = keep_ref.shape[1]
    total = TEAM * rows
    picked = total // 8
    own_b = pl.ds(head, picked, stride=8)

    blocks = [keep_ref[0], recv_ref[0]]
    for ref in (r1, r2, r3):
        blocks += [ref[:rows], ref[rows:]]
    for i, block in enumerate(blocks):
        at = slice(i * rows, (i + 1) * rows)
        keys[at] = block[:, :D]
        vals[at] = block[:, D : 2 * D]
        xa[at] = block[:, : 2 * D].astype(F32)
        xb[at] = block[:, 2 * D :].astype(F32)
    kvt[...] = xa[...].T.astype(BF16)
    flipped = xb[...].T
    qt[...] = flipped[:D].astype(BF16)
    gt[...] = flipped[D:]

    mine = xb[own_b, :].astype(BF16)
    team = my_team()
    pieces = [xa[own_b, :]]
    for j in range(1, near + far + 1):
        slot = pl.ds((team ^ j) * TEAM, TEAM)
        for i in range(rows // 64 if j <= near else 1):
            part = slots_ref[slot, :, i * 2 * D : (i + 1) * 2 * D]
            pieces.append(part.astype(F32).reshape(-1, 2 * D))
    other = jnp.concatenate(pieces, axis=0).astype(BF16)
    kext, vext = other[:, :D], other[:, D:]
    q_b, g_b = mine[:, :D], mine[:, D:]
    extent = other.shape[0]
    row = lax.broadcasted_iota(jnp.int32, (extent, 1), 0)
    use_b = row < (near + 1) * picked
    use_c = lax.rem(row, 8) < jnp.where(use_b, 1, rows // 64)
    scores = dot_t(kext, q_b)

    def branch(use):
        masked = jnp.where(use, scores, NONE)
        highest = jnp.max(masked, axis=0, keepdims=True)
        exps = jnp.exp(masked - highest)
        mass = jnp.sum(exps, axis=0, keepdims=True)
        probs = (exps * (1.0 / mass)).astype(BF16)
        return highest + jnp.log(mass), highest, exps, probs

    level_b, highest_b, exps_b, probs_b = branch(use_b)
    level_c, highest_c, exps_c, probs_c = branch(use_c)
    vext_t = vext.astype(F32).T.astype(BF16)
    kext_t = kext.astype(F32).T.astype(BF16)
    part_b = dot(vext_t, probs_b)
    part_c = dot(vext_t, probs_c)
    lane = lax.broadcasted_iota(jnp.int32, (1, picked), 1)
    in_c = lax.rem(lane, 8) == 0
    level_in = jnp.where(in_c, level_c, NONE)
    top = jnp.maximum(level_b, level_in)
    level_bc = top + jnp.log(jnp.exp(level_b - top) + jnp.exp(level_in - top))
    part_bc = jnp.exp(level_b - level_bc) * part_b + jnp.exp(level_in - level_bc) * part_c
    lanes = lax.broadcasted_iota(jnp.int32, z.shape, 1)
    z[...] = jnp.where(lanes < D, 0.0, NONE)
    z[own_b, :] = jnp.concatenate([part_bc, jnp.broadcast_to(level_bc, (D, picked))], axis=0).T
    zt[...] = z[...].T

    tile = total
    chunk = 2 * rows
    dkv[...] = jnp.zeros_like(dkv)
    zero = jnp.zeros((D, tile), BF16)

    def fold(x, op):
        return op(x.reshape(-1, 8, x.shape[1]), axis=0)

    def one_tile(t, carry):
        here = pl.ds(pl.multiple_of(t * tile, tile), tile)
        q_t = qt[:, here]
        top = jnp.full((8, tile), NONE, F32)
        for at in range(0, total, chunk):
            s = dot(keys[at : at + chunk, :], q_t)
            st[at : at + chunk, :] = s
            top = jnp.maximum(top, fold(s, jnp.max))
        top = jnp.max(top, axis=0, keepdims=True)
        mass = jnp.zeros((8, tile), F32)
        for at in range(0, total, chunk):
            e = jnp.exp(st[at : at + chunk, :] - top)
            st[at : at + chunk, :] = e
            mass = mass + fold(e, jnp.sum)
        mass = jnp.sum(mass, axis=0, keepdims=True)
        level = top + jnp.log(mass)
        norm = 1.0 / mass
        part = [jnp.zeros((D, tile), F32)] * 2
        for i, at in enumerate(range(0, total, chunk)):
            probs = (st[at : at + chunk, :] * norm).astype(BF16)
            part[i % 2] = part[i % 2] + dot(kvt[D:, at : at + chunk], probs)
        level_o = zt[D : D + 1, here]
        highest = jnp.maximum(level, level_o)
        overall = highest + jnp.log(jnp.exp(level - highest) + jnp.exp(level_o - highest))
        weight = jnp.exp(level - overall)
        combined = weight * (part[0] + part[1]) + jnp.exp(level_o - overall) * zt[:D, here]
        g_t = gt[:, here]
        align = jnp.sum(g_t * combined, axis=0, keepdims=True)
        low = level.astype(BF16).astype(F32)
        factor = jnp.exp(low - level) * weight
        grads = (factor * g_t).astype(BF16)
        corr = (factor * align).astype(BF16).astype(F32)
        lift = jnp.exp(top - low)
        right = jnp.concatenate(
            [jnp.concatenate([q_t, zero], axis=1), jnp.concatenate([zero, grads], axis=1)], axis=0
        )
        dq = [jnp.zeros((D, tile), F32)] * 2
        for i, at in enumerate(range(0, total, chunk)):
            redo = st[at : at + chunk, :] * lift
            dprob = dot(vals[at : at + chunk, :], grads)
            dscore = (redo * (dprob - corr)).astype(BF16)
            dq[i % 2] = dq[i % 2] + dot(kvt[:D, at : at + chunk], dscore)
            dkv[at : at + chunk, :] += dot_t(
                jnp.concatenate([dscore, redo.astype(BF16)], axis=1), right
            )
        oq[here, :] = jnp.concatenate([combined, (dq[0] + dq[1]) * SCALE], axis=0).T
        stats[here, :] = jnp.concatenate(
            [align, overall, jnp.zeros((126, tile), F32)], axis=0
        ).T
        return carry

    lax.fori_loop(0, total // tile, one_tile, 0)

    numbers = stats[own_b, :]
    align, overall = numbers[:, 0:1], numbers[:, 1:2]
    g32 = g_b.astype(F32)
    levels_t = jnp.concatenate(
        [level_b, level_c, level_in, jnp.zeros((125, picked), F32)], axis=0
    ).T
    dk = jnp.zeros((extent, D), F32)
    dv = jnp.zeros((extent, D), F32)
    dq = jnp.zeros((D, picked), F32)
    for level, weight, highest, exps in (
        (levels_t[:, 0:1], jnp.exp(levels_t[:, 0:1] - overall), highest_b, exps_b),
        (levels_t[:, 1:2], jnp.exp(levels_t[:, 2:3] - overall), highest_c, exps_c),
    ):
        low = level.astype(BF16).astype(F32)
        factor = jnp.exp(low - level) * weight
        grads = (factor * g32).astype(BF16)
        corr = (factor * align).astype(BF16).astype(F32)
        column_id = lax.broadcasted_iota(jnp.int32, (picked, 2 * D), 1)
        across = jnp.where(column_id == 0, corr, low).T
        redo = exps * jnp.exp(highest - across[1:2])
        dscore = (redo * (dot_t(vext, grads) - across[0:1])).astype(BF16)
        dk = dk + dot(dscore, q_b)
        dv = dv + dot(redo.astype(BF16), grads)
        dq = dq + dot(kext_t, dscore)
    both = jnp.concatenate([dk, dv], axis=1)
    dkv[own_b, :] = dkv[own_b, :] + both[:picked]
    oq[own_b, :] = oq[own_b, :] + jnp.concatenate([jnp.zeros_like(dq), dq * SCALE], axis=0).T
    parts_ref[...] = jnp.zeros_like(parts_ref)
    at = picked
    for j in range(1, near + far + 1):
        slot = pl.ds((team ^ j) * TEAM, TEAM)
        for i in range(rows // 64 if j <= near else 1):
            piece = both[at : at + 8 * TEAM].reshape(TEAM, 8, 2 * D)
            parts_ref[slot, :, i * 2 * D : (i + 1) * 2 * D] = piece.astype(BF16)
            at += 8 * TEAM
    out = pltpu.make_async_copy(parts_ref, parts_hbm, sems.at[0])
    out.start()
    for t, ref in enumerate((o0, o1, o2, o3)):
        at = slice(2 * t * rows, 2 * (t + 1) * rows)
        ref[:, : 2 * D] = dkv[at, :].astype(BF16)
        ref[:, 2 * D :] = oq[at, :].astype(BF16)
    out.wait()


def middle_body(m0, m3, m1, m2, keep_ref, send_ref):
    rows = keep_ref.shape[1]
    for t, main in enumerate((m0, m1, m2, m3)):
        keep_ref[t] = main[:rows]
        send_ref[t] = main[rows:]


def order_body(keep_ref, out_ref):
    chip, column = place()
    for i in range(3):
        out_ref[i] = keep_ref[(i + column) ^ chip]


def unpack_body(
    near,
    keep_ref,
    recv_ref,
    parts_ref,
    out_hbm,
    dq_hbm,
    dk_hbm,
    dv_hbm,
    heads_ref,
    wide,
    ready,
    sems,
):
    chip, column = place()
    for side in range(2):

        @pl.when(column == side)
        def _():
            for h in range(HEADS):
                if h // 3 == side:
                    heads_ref[h] = keep_ref[h % 3]
                else:
                    heads_ref[h] = recv_ref[(h % 3 + h // 3) ^ chip]

    leaving = []

    def leave(value, target):
        i = len(leaving)
        ready[i] = value
        leaving.append(pltpu.make_async_copy(ready.at[i], target, sems.at[i]))
        leaving[i].start()

    for at, target in ((2, out_hbm), (3, dq_hbm)):
        leave(
            jnp.concatenate([heads_ref[h, :, at * D : (at + 1) * D] for h in range(HEADS)], axis=1),
            target,
        )
    rows = keep_ref.shape[1]
    team = my_team()
    teams = parts_ref.shape[0] // TEAM
    for h in range(HEADS):
        wide[h] = heads_ref[h, :, : 2 * D].astype(F32)
    for h in range(HEADS):
        member = 2 * (h % 3 + h // 3) + h // 3
        for j in range(1, teams):
            part = parts_ref[(team ^ j) * TEAM + member].astype(F32)
            pieces = [part[:, i * 2 * D : (i + 1) * 2 * D] for i in range(rows // 64)]
            if j <= near:
                chosen, part = pl.ds(h, rows // 8, stride=8), jnp.concatenate(pieces, axis=0)
            else:
                chosen, part = pl.ds(h, rows // 64, stride=64), pieces[0][: rows // 64]
            wide[h, chosen, :] = wide[h, chosen, :] + part
    for at, target in ((0, dk_hbm), (1, dv_hbm)):
        leave(
            jnp.concatenate(
                [wide[h, :, at * D : (at + 1) * D] for h in range(HEADS)], axis=1
            ).astype(BF16),
            target,
        )
    for copy in leaving:
        copy.wait()


def shards(query_rows, key_rows, value_rows, out_grad):
    rows = query_rows.shape[0]
    width = 4 * D
    count = lax.axis_size("outer") * lax.axis_size("inner")
    near = 2 * lax.axis_size("inner") // TEAM - 1
    far = count // TEAM - 1 - near
    to_owner = lambda source, target: owns(target)
    from_owner = lambda source, target: owns(source)
    total = TEAM * rows

    block = ((4, rows, width), BF16)
    slots_shape = ((count, 8, rows // 64 * 2 * D), BF16)
    given = pltpu.VMEM((rows, HEADS * D), BF16)
    keep, send, slots = call(
        functools.partial(pack_body, near),
        [block, block, slots_shape],
        *[pltpu.with_memory_space_constraint(x, pltpu.HBM) for x in (query_rows, key_rows, value_rows, out_grad)],
        scratch=[pltpu.VMEM((HEADS, rows, width), BF16)] + [given] * 4
        + [
            pltpu.VMEM((rows, 2 * D), F32),
            pltpu.VMEM((64, 2 * D), F32),
            pltpu.VMEM((2, HEADS, 8, rows // 64 * 2 * D), BF16),
            pltpu.VMEM(*slots_shape),
            pltpu.SemaphoreType.DMA((5,)),
        ],
        specs=[HBM] * 4,
        outs_in=[VMEM, VMEM, HBM],
    )
    recv = move(send, 1)
    s1, s2, s3 = call(regroup_body, [((2 * rows, width), BF16)] * 3, keep, recv)
    got = [move(s, 2 * t, to_owner) for t, s in ((1, s1), (2, s2), (3, s3))]
    slots = lax.all_to_all(slots, AXES, 0, 0)
    *mains, parts = call(
        functools.partial(main_body, near, far),
        [((2 * rows, width), BF16)] * 4 + [slots_shape],
        keep,
        recv,
        got[1],
        got[0],
        got[2],
        slots,
        scratch=[
            pltpu.VMEM((total, 2 * D), F32),
            pltpu.VMEM((total, 2 * D), F32),
            pltpu.VMEM((total, D), BF16),
            pltpu.VMEM((total, D), BF16),
            pltpu.VMEM((D, total), BF16),
            pltpu.VMEM((D, total), F32),
            pltpu.VMEM((2 * D, total), BF16),
            pltpu.VMEM((total, total), F32),
            pltpu.VMEM((total, 2 * D), F32),
            pltpu.VMEM((total, 2 * D), F32),
            pltpu.VMEM((total, 2 * D), F32),
            pltpu.VMEM((2 * D, total), F32),
            pltpu.VMEM((total, 2 * D), F32),
            pltpu.VMEM(*slots_shape),
            pltpu.SemaphoreType.DMA((1,)),
        ],
        outs_in=[VMEM] * 4 + [HBM],
    )
    back = [mains[0]] + [move(mains[t], 2 * t, from_owner) for t in (1, 2, 3)]
    parts = lax.all_to_all(parts, AXES, 0, 0)
    keep, send = call(
        middle_body, [block, block], back[0], back[3], back[1], back[2], cost=HINT
    )
    recv = move(send, 1)
    (mine,) = call(order_body, [((3, rows, width), BF16)], keep, cost=HINT)
    out = ((rows, HEADS * D), BF16)
    return tuple(
        call(
            functools.partial(unpack_body, near), [out] * 4, mine, recv, parts,
            scratch=[
                pltpu.VMEM((HEADS, rows, width), BF16),
                pltpu.VMEM((HEADS, rows, 2 * D), F32),
                pltpu.VMEM((4, rows, HEADS * D), BF16),
                pltpu.SemaphoreType.DMA((4,)),
            ],
            outs_in=[HBM] * 4,
        )
    )


def solution(mesh):
    spec = P(AXES, None)
    return jax.shard_map(
        shards, mesh=mesh, in_specs=(spec,) * 4, out_specs=(spec,) * 4, check_vma=False
    )
```
